512 devices in a mesh: lat: 32 (over z, core), ch: 16 (over y, x).
Axes of the slice: x: 4, y: 4, z: 16, core: 2. Of those that a mesh axis runs over, the one named last changes fastest.
Arguments:
- fields: bfloat16 [2, 704, 32, 1440], P(None, 'lat', 'ch'), may hold values from -6 to 6
- table: bfloat16 [704, 704, 352], P('lat', 'ch'), may hold values from -1 to 1, as said below
Outputs:
- coefficients: float32 [704, 704, 128], P('lat', 'ch')
The draws below stay inside these ranges and needn't reach their ends.
Inputs may be any that keep to these rules, and one draw needn't show every extreme that they name: table[m, l, k] is zero wherever l < m.
All inputs are finite; a program needn't handle non-finite values.
Results may differ from the reference program's by a relative error of at most 0.005.
Values may be sent and summed in bfloat16 or wider, within the bound.
A program may use at most 64 MiB of HBM per device.

```python
import math
import jax
import jax.numpy as jnp
from jax import lax

NLAT = 704
NLON = 1440
MODES = 704
CH = 32
BATCH = 2
HALF = 352


def draw_table(key, part):
    values = jax.random.truncated_normal(key, -4.0, 4.0, (MODES, MODES, HALF), jnp.float32) * HALF ** (-0.5)
    degree = jnp.arange(MODES, dtype=jnp.int32)[None, :, None]
    order = jnp.arange(MODES, dtype=jnp.int32)[:, None, None]
    return jnp.where(degree >= order, values, 0.0).astype(jnp.bfloat16)


def block_scale(rng, dims, cuts, smallest, largest):
    level = 1.0
    for dim, blocks in cuts:
        heights = jax.random.uniform(jax.random.fold_in(jax.random.fold_in(rng, 6), dim), (blocks,), jnp.float32, smallest / len(cuts), largest / len(cuts))
        level = level * jnp.repeat(jnp.exp(heights), dims[dim] // blocks).reshape((-1,) + (1,) * (len(dims) - 1 - dim))
    return level


def gaussian(rng, shape, width, limit, pieces=(), kind=jnp.bfloat16):
    values = width * jax.random.normal(rng, shape, jnp.float32)
    if pieces:
        values = values * block_scale(rng, shape, pieces, -0.22, 0.18)
    return jnp.clip(values, -limit, limit).astype(kind)


def setup_inputs(seed: int = 0) -> dict:
    arg_keys = jax.random.split(jax.random.key(seed), 3)
    fields = gaussian(arg_keys[0], (BATCH, NLAT, CH, NLON), 1.0, 6.0, ((1, 32), (2, 16)))
    table = draw_table(jax.random.fold_in(arg_keys[2], 71), 0)
    return dict(fields=fields, table=table)


def fourier_table(nlon, modes):
    cols = jnp.arange(nlon, dtype=jnp.int32)[:, None]
    orders = jnp.arange(modes, dtype=jnp.int32)[None, :]
    phase = (cols * orders % nlon).astype(jnp.float32) * (2.0 * math.pi / nlon)
    factor = 1.0 / math.sqrt(nlon)
    return jnp.concatenate([jnp.cos(phase) * factor, -jnp.sin(phase) * factor], axis=1).astype(jnp.bfloat16)

def reference(fields, table):
    fourier = fourier_table(NLON, MODES)

    def transform(sample):
        flat = sample.reshape(NLAT * CH, NLON)
        return jnp.dot(flat, fourier, preferred_element_type=jnp.float32).astype(jnp.bfloat16).reshape(NLAT, CH, 2, MODES)
    spectrum = lax.map(transform, fields)
    north = spectrum[:, :HALF].astype(jnp.float32)
    south = spectrum[:, HALF:][:, ::-1].astype(jnp.float32)
    parts = jnp.concatenate([(north + south).astype(jnp.bfloat16), (north - south).astype(jnp.bfloat16)], axis=1)
    per_order = jnp.transpose(parts, (4, 1, 0, 2, 3)).reshape(MODES, NLAT, BATCH * CH * 2)
    degrees = jnp.arange(MODES, dtype=jnp.int32)[:, None]

    def one_order(items):
        tab_m, par_m, order = items
        even = (degrees - order) % 2 == 0
        zero = jnp.zeros_like(tab_m)
        doubled = jnp.concatenate([jnp.where(even, tab_m, zero), jnp.where(even, zero, tab_m)], axis=1)
        return jnp.dot(doubled, par_m, preferred_element_type=jnp.float32)
    return lax.map(one_order, (table, per_order, jnp.arange(MODES, dtype=jnp.int32)))
```

```python
import functools
import math

import numpy as np
import jax
import jax.numpy as jnp
from jax import lax
from jax.experimental import pallas as pl
from jax.experimental.pallas import tpu as pltpu
from jax.sharding import PartitionSpec as P

NLON = 1440
FOLD = NLON // 2
NZ = 16
NLATDEV = 32
SLAB = 22
LBLK = 44
HALF = 352
GROUPS = 3
LP = 48
KP = 384
FP = 768
MESH = pl.DeviceIdType.MESH
NT = (((1,), (1,)), ((), ()))


def slots(g):
    return min(4, SLAB // 2 - 4 * g)


def order_of(g, par, j):
    return 2 * (4 * g + j) + par


def fourier_rows():
    table = np.zeros((GROUPS, 2, NLATDEV, 4, 2, FP), np.float64)
    cols = np.arange(FOLD, dtype=np.int64)
    scale = 1.0 / math.sqrt(NLON)
    owners = np.arange(NLATDEV, dtype=np.int64)[:, None]
    for g in range(GROUPS):
        for par in range(2):
            for j in range(slots(g)):
                order = owners * SLAB + order_of(g, par, j)
                angle = (order * cols[None, :] % NLON) * (2.0 * math.pi / NLON)
                table[g, par, :, j, 0, :FOLD] = np.cos(angle) * scale
                table[g, par, :, j, 1, :FOLD] = -np.sin(angle) * scale
    return table.reshape(GROUPS, 2, NLATDEV * 8, FP).astype(jnp.bfloat16)


def kernel(
    x_ref, f_ref, t_ref, out_ref,
    fv, tv, sb, rb, tg, yf, yp, wb, ob, orr, pm,
    in_sem, z_send, z_recv, t_send, t_recv, p_send, p_recv, o_send, o_recv,
):
    f32, bf16 = jnp.float32, jnp.bfloat16
    lat = lax.axis_index("lat")
    ch = lax.axis_index("ch")
    z, core = lat // 2, lat % 2
    y, x = ch // 4, ch % 4

    f_copy = pltpu.make_async_copy(f_ref, fv, in_sem.at[0])
    t_copy = pltpu.make_async_copy(t_ref, tv, in_sem.at[1])
    f_copy.start()
    t_copy.start()

    def peer(t):
        u, h = t // 2, t % 2
        dz = jnp.where(u % 2 == 1, 8 - (u + 1) // 2, 8 + u // 2)
        return ((z + dz) % NZ) * 2 + (core + 1 + h) % 2

    pq = ((x, y), (y, x))

    def ch_at(par, p, q):
        return q * 4 + p if par == 0 else p * 4 + q

    barrier = pltpu.get_barrier_semaphore()

    def greet(t, carry):
        pl.semaphore_signal(barrier, inc=1, device_id={"lat": peer(t)}, device_id_type=MESH)
        return carry

    lax.fori_loop(0, NLATDEV - 1, greet, 0)
    for d in range(1, 4):
        for par in range(2):
            p, q = pq[par]
            pl.semaphore_signal(
                barrier, inc=1, device_id={"ch": ch_at(par, (p + d) % 4, q)}, device_id_type=MESH
            )

    dst = lax.broadcasted_iota(jnp.int32, (128, 96), 0)
    src = lax.broadcasted_iota(jnp.int32, (128, 96), 1)
    one = jnp.ones_like(dst)
    zero = jnp.zeros_like(dst)
    bc = (
        jnp.where(dst >= SLAB, one, zero)
        + jnp.where(dst >= 2 * SLAB, one, zero)
        + jnp.where(dst >= 3 * SLAB, one, zero)
    )
    k = dst - SLAB * bc
    south = jnp.where(lat >= NLATDEV // 2, 1, 0)
    k = k + south * (SLAB - 1 - 2 * k)
    want = (bc // 2) * (2 * SLAB) + 2 * k + bc % 2
    hit = jnp.logical_and(want == src, dst < 4 * SLAB)
    perm = jnp.where(hit, 1.0, 0.0).astype(bf16)
    xp = [
        jnp.dot(perm, x_ref[par], preferred_element_type=f32).astype(bf16) for par in range(2)
    ]

    f_copy.wait()
    for g in range(GROUPS):
        halves = [
            lax.dot_general(fv[g, par], xp[par], NT, preferred_element_type=f32).reshape(
                NLATDEV, 8, 128
            )
            for par in range(2)
        ]
        sb[g] = jnp.concatenate(halves, axis=1).astype(bf16)
        rb[g, lat] = sb[g, lat]

    t_copy.wait()
    for g in range(GROUPS):
        for par in range(2):
            c = 2 * g + par
            q = pq[par][1]
            tg[c, q] = jnp.zeros((4, LP, KP), bf16)
            if slots(g) < 4:
                for i in range(4):
                    tg[c, i, 3] = jnp.zeros((LP, KP), bf16)
            for j in range(slots(g)):
                tg[c, q, j, :LBLK, :HALF] = tv[order_of(g, par, j)]

    pl.semaphore_wait(barrier, NLATDEV - 1 + 6)

    def z_copy(g, t):
        dest = peer(t)
        return pltpu.make_async_remote_copy(
            src_ref=sb.at[g, dest],
            dst_ref=rb.at[g, lat],
            send_sem=z_send.at[g, dest],
            recv_sem=z_recv.at[g, lat],
            device_id={"lat": dest},
            device_id_type=MESH,
        )

    def z_arrival(g, t):
        source = peer(t)
        return pltpu.make_async_remote_copy(
            src_ref=sb.at[g, source],
            dst_ref=rb.at[g, source],
            send_sem=z_send.at[g, source],
            recv_sem=z_recv.at[g, source],
            device_id={"lat": source},
            device_id_type=MESH,
        )

    for g in range(GROUPS):

        def send(t, carry, g=g):
            z_copy(g, t).start()
            return carry

        lax.fori_loop(0, NLATDEV - 1, send, 0)

    def t_move(c, d):
        g, par = c // 2, c % 2
        p, q = pq[par]
        to, n = (q + d) % 4, slots(g)
        return pltpu.make_async_remote_copy(
            src_ref=tg.at[c, q, pl.ds(0, n)],
            dst_ref=tg.at[c, q, pl.ds(0, n)],
            send_sem=t_send.at[c, d],
            recv_sem=t_recv.at[c, d],
            device_id={"ch": ch_at(par, p, to)},
            device_id_type=MESH,
        )

    def t_arrival(c, d):
        g, par = c // 2, c % 2
        p, q = pq[par]
        frm, n = (q + 4 - d) % 4, slots(g)
        return pltpu.make_async_remote_copy(
            src_ref=tg.at[c, frm, pl.ds(0, n)],
            dst_ref=tg.at[c, frm, pl.ds(0, n)],
            send_sem=t_send.at[c, d],
            recv_sem=t_recv.at[c, d],
            device_id={"ch": ch_at(par, p, frm)},
            device_id_type=MESH,
        )

    def p_move(c, d):
        p, q = pq[c % 2]
        return pltpu.make_async_remote_copy(
            src_ref=yp.at[c],
            dst_ref=wb.at[c, :, p],
            send_sem=p_send.at[c, d],
            recv_sem=p_recv.at[c, d],
            device_id={"ch": ch_at(c % 2, (p + d) % 4, q)},
            device_id_type=MESH,
        )

    def p_arrival(c, d):
        p, q = pq[c % 2]
        frm = (p + 4 - d) % 4
        return pltpu.make_async_remote_copy(
            src_ref=yp.at[c],
            dst_ref=wb.at[c, :, frm],
            send_sem=p_send.at[c, d],
            recv_sem=p_recv.at[c, d],
            device_id={"ch": ch_at(c % 2, frm, q)},
            device_id_type=MESH,
        )

    def o_move(c, d):
        p, q = pq[c % 2]
        to = (q + d) % 4
        return pltpu.make_async_remote_copy(
            src_ref=ob.at[c, to],
            dst_ref=orr.at[c, q],
            send_sem=o_send.at[c, d],
            recv_sem=o_recv.at[c, d],
            device_id={"ch": ch_at(c % 2, p, to)},
            device_id_type=MESH,
        )

    def o_arrival(c, d):
        p, q = pq[c % 2]
        frm = (q + 4 - d) % 4
        return pltpu.make_async_remote_copy(
            src_ref=ob.at[c, frm],
            dst_ref=orr.at[c, frm],
            send_sem=o_send.at[c, d],
            recv_sem=o_recv.at[c, d],
            device_id={"ch": ch_at(c % 2, p, frm)},
            device_id_type=MESH,
        )

    for c in range(2 * GROUPS):
        for d in (1, 3, 2):
            t_move(c, d).start()

    for par in range(2):
        row = lax.broadcasted_iota(jnp.int32, (512, 512), 0)
        col = lax.broadcasted_iota(jnp.int32, (512, 512), 1)
        qq, pp = row // 128, (row // 32) % 4
        chan = ch_at(par, pp, qq)
        want = (
            ((row // 2) % 4) * 128
            + ((row // 16) % 2) * 64
            + chan * 4
            + ((row // 8) % 2) * 2
            + row % 2
        )
        pm[par] = jnp.where(want == col, 1.0, 0.0).astype(bf16)

    lane = lax.broadcasted_iota(jnp.int32, (16, 128), 1)

    def unpack(g):
        def arrived(t, carry):
            z_arrival(g, t).wait_recv()
            return carry

        lax.fori_loop(0, NLATDEV - 1, arrived, 0)
        for b in range(4):
            acc = [[jnp.zeros((16, 128), f32) for _ in range(3)] for _ in range(2)]
            for s in range(NLATDEV // 2):
                north = rb[g, s].astype(f32)
                other = rb[g, NLATDEV - 1 - s].astype(f32)
                first = SLAB * s
                shift = (first - SLAB * b) % 128
                for i, val in enumerate((north + other, north - other)):
                    if shift:
                        val = pltpu.roll(val, shift, 1)
                    for t in range(first // 128, (first + SLAB - 1) // 128 + 1):
                        lo, hi = first - 128 * t, first + SLAB - 128 * t
                        inside = jnp.logical_and(lane >= lo, lane < hi)
                        acc[i][t] = jnp.where(inside, val, acc[i][t])
            for par in range(2):
                for i in range(2):
                    for t in range(3):
                        yf[par, i, b, :, 128 * t : 128 * t + 128] = acc[i][t][
                            8 * par : 8 * par + 8
                        ]
        for par in range(2):
            c = 2 * g + par
            block = yf[par].reshape(2, 32, KP).astype(bf16)
            yp[c] = block
            wb[c, :, pq[par][0]] = block
            for d in (1, 3, 2):
                p_move(c, d).start()

    rows = lax.broadcasted_iota(jnp.int32, (LP, 128), 0)
    lanes = lax.broadcasted_iota(jnp.int32, (LP, 128), 1)
    lane_slot = (lanes // 2) % 4

    def project(c):
        g, par = c // 2, c % 2
        q = pq[par][1]
        for d in (1, 3, 2):
            t_arrival(c, d).wait_recv()
        for d in (1, 3, 2):
            p_arrival(c, d).wait_recv()
        got = lax.dot_general(
            tg[c].reshape(16 * LP, KP),
            wb[c].reshape(256, KP),
            NT,
            preferred_element_type=f32,
        )
        same = rows % 2 == par
        for i in range(4):
            total = jnp.zeros((LP, 128), f32)
            for j in range(slots(g)):
                lo = (4 * i + j) * LP
                both = got[lo : lo + LP]
                val = jnp.where(same, both[:, :128], both[:, 128:])
                total = jnp.where(lane_slot == j, val, total)
            ob[c, i] = total.astype(bf16)
        orr[c, q] = ob[c, q]
        for d in (1, 3, 2):
            o_move(c, d).start()

    def finish(c):
        g, par = c // 2, c % 2
        for d in (1, 3, 2):
            o_arrival(c, d).wait_recv()
        full = jnp.concatenate([orr[c, i] for i in range(4)], axis=1)
        res = jnp.dot(full, pm[par], preferred_element_type=f32)
        for j in range(slots(g)):
            out_ref[order_of(g, par, j)] = res[:LBLK, 128 * j : 128 * j + 128]

    for g in range(GROUPS):
        unpack(g)
        for par in range(2):
            project(2 * g + par)
        if g:
            for par in range(2):
                finish(2 * (g - 1) + par)
    for par in range(2):
        finish(2 * (GROUPS - 1) + par)

    for g in range(GROUPS):

        def sent(t, carry, g=g):
            z_copy(g, t).wait_send()
            return carry

        lax.fori_loop(0, NLATDEV - 1, sent, 0)
    for c in range(2 * GROUPS):
        for d in range(1, 4):
            t_move(c, d).wait_send()
            p_move(c, d).wait_send()
            o_move(c, d).wait_send()


def shards(fields, table):
    wide = fields.astype(jnp.float32)
    first, second = wide[..., :FOLD], wide[..., FOLD:]
    folded = jnp.stack([first + second, first - second]).astype(jnp.bfloat16)
    folded = folded.reshape(2, 4 * SLAB, FOLD)
    folded = jnp.pad(folded, ((0, 0), (0, 96 - 4 * SLAB), (0, FP - FOLD)))
    fourier = jnp.asarray(fourier_rows())
    bf16, f32 = jnp.bfloat16, jnp.float32
    dma = pltpu.SemaphoreType.DMA
    chunks = 2 * GROUPS
    return pl.pallas_call(
        kernel,
        out_shape=jax.ShapeDtypeStruct((SLAB, LBLK, 128), f32),
        in_specs=[
            pl.BlockSpec(memory_space=pltpu.VMEM),
            pl.BlockSpec(memory_space=pl.ANY),
            pl.BlockSpec(memory_space=pl.ANY),
        ],
        out_specs=pl.BlockSpec(memory_space=pltpu.VMEM),
        scratch_shapes=[
            pltpu.VMEM((GROUPS, 2, NLATDEV * 8, FP), bf16),
            pltpu.VMEM((SLAB, LBLK, HALF), bf16),
            pltpu.VMEM((GROUPS, NLATDEV, 16, 128), bf16),
            pltpu.VMEM((GROUPS, NLATDEV, 16, 128), bf16),
            pltpu.VMEM((chunks, 4, 4, LP, KP), bf16),
            pltpu.VMEM((2, 2, 4, 8, KP), f32),
            pltpu.VMEM((chunks, 2, 32, KP), bf16),
            pltpu.VMEM((chunks, 2, 4, 32, KP), bf16),
            pltpu.VMEM((chunks, 4, LP, 128), bf16),
            pltpu.VMEM((chunks, 4, LP, 128), bf16),
            pltpu.VMEM((2, 512, 512), bf16),
            dma((2,)),
            dma((GROUPS, NLATDEV)),
            dma((GROUPS, NLATDEV)),
            dma((chunks, 4)),
            dma((chunks, 4)),
            dma((chunks, 4)),
            dma((chunks, 4)),
            dma((chunks, 4)),
            dma((chunks, 4)),
        ],
        compiler_params=pltpu.CompilerParams(
            collective_id=0, has_side_effects=True, vmem_limit_bytes=48 << 20
        ),
    )(folded, fourier, table)


def solution(mesh):
    return jax.shard_map(
        shards,
        mesh=mesh,
        in_specs=(P(None, "lat", "ch", None), P("lat", "ch", None)),
        out_specs=P("lat", "ch", None),
        check_vma=False,
    )
```

```python
import functools
import math

import numpy as np
import jax
import jax.numpy as jnp
from jax import lax
from jax.experimental import pallas as pl
from jax.experimental.pallas import tpu as pltpu
from jax.sharding import PartitionSpec as P

NLON = 1440
FOLD = NLON // 2
NZ = 16
NLATDEV = 32
SLAB = 22
LBLK = 44
HALF = 352
GROUPS = 3
LP = 48
KP = 384
FP = 768
MESH = pl.DeviceIdType.MESH
NT = (((1,), (1,)), ((), ()))


def slots(g):
    return min(4, SLAB // 2 - 4 * g)


def order_of(g, par, j):
    return 2 * (4 * g + j) + par


def fourier_rows():
    table = np.zeros((GROUPS, 2, NLATDEV, 4, 2, FP), np.float64)
    cols = np.arange(FOLD, dtype=np.int64)
    scale = 1.0 / math.sqrt(NLON)
    owners = np.arange(NLATDEV, dtype=np.int64)[:, None]
    for g in range(GROUPS):
        for par in range(2):
            for j in range(slots(g)):
                order = owners * SLAB + order_of(g, par, j)
                angle = (order * cols[None, :] % NLON) * (2.0 * math.pi / NLON)
                table[g, par, :, j, 0, :FOLD] = np.cos(angle) * scale
                table[g, par, :, j, 1, :FOLD] = -np.sin(angle) * scale
    return table.reshape(GROUPS, 2, NLATDEV * 8, FP).astype(jnp.bfloat16)


def kernel(
    x_ref, f_ref, t_ref, out_ref,
    xv, xs, fv, tv, sb, rb, tg, yf, yp, wb, ob, orr, pm,
    in_sem, z_send, z_recv, t_send, t_recv, p_send, p_recv, o_send, o_recv,
):
    f32, bf16 = jnp.float32, jnp.bfloat16
    lat = lax.axis_index("lat")
    ch = lax.axis_index("ch")
    z, core = lat // 2, lax.rem(lat, 2)
    y, x = ch // 4, lax.rem(ch, 4)

    x_copy = pltpu.make_async_copy(x_ref, xv, in_sem.at[0])
    f_copy = pltpu.make_async_copy(f_ref, fv, in_sem.at[1])
    t_copy = pltpu.make_async_copy(t_ref, tv, in_sem.at[2])
    x_copy.start()
    f_copy.start()
    t_copy.start()

    hops = [8 - (u + 1) // 2 if u % 2 else 8 + u // 2 for u in range(NZ)]
    peers = [lax.rem(z + dz, NZ) * 2 + at for dz in hops for at in (1 - core, core)][:-1]

    pq = ((x, y), (y, x))

    def ch_at(par, p, q):
        return q * 4 + p if par == 0 else p * 4 + q

    barrier = pltpu.get_barrier_semaphore()

    for peer in peers:
        pl.semaphore_signal(barrier, inc=1, device_id={"lat": peer}, device_id_type=MESH)
    for d in range(1, 4):
        for par in range(2):
            p, q = pq[par]
            pl.semaphore_signal(
                barrier, inc=1, device_id={"ch": ch_at(par, lax.rem(p + d, 4), q)}, device_id_type=MESH
            )

    dst = lax.broadcasted_iota(jnp.int32, (128, 96), 0)
    src = lax.broadcasted_iota(jnp.int32, (128, 96), 1)
    one = jnp.ones_like(dst)
    zero = jnp.zeros_like(dst)
    bc = (
        jnp.where(dst >= SLAB, one, zero)
        + jnp.where(dst >= 2 * SLAB, one, zero)
        + jnp.where(dst >= 3 * SLAB, one, zero)
    )
    k = dst - SLAB * bc
    south = jnp.where(lat >= NLATDEV // 2, 1, 0)
    k = k + south * (SLAB - 1 - 2 * k)
    want = (bc // 2) * (2 * SLAB) + 2 * k + bc % 2
    hit = jnp.logical_and(want == src, dst < 4 * SLAB)
    perm = jnp.where(hit, 1.0, 0.0).astype(bf16)
    xs[4 * SLAB :, :] = jnp.zeros((8, 2 * FP), f32)
    xs[:, NLON:] = jnp.zeros((96, 2 * FP - NLON), f32)
    x_copy.wait()
    for i in range(2 * SLAB):
        xs[2 * i : 2 * i + 2, :NLON] = xv[i // SLAB, i % SLAB].astype(f32)
    whole = xs[...]
    first = whole[:, :FP]
    second = pltpu.roll(whole, 2 * FP - FOLD, 1)[:, :FP]
    xp = [
        jnp.dot(perm, val.astype(bf16), preferred_element_type=f32).astype(bf16)
        for val in (first + second, first - second)
    ]

    f_copy.wait()

    def transform(g):
        halves = [
            lax.dot_general(fv[g, par], xp[par], NT, preferred_element_type=f32).reshape(
                NLATDEV, 8, 128
            )
            for par in range(2)
        ]
        sb[g] = jnp.stack(halves, axis=1).astype(bf16)
        rb[g, lat] = sb[g, lat]

    def z_copy(g, dest):
        n = 2 * slots(g)
        return pltpu.make_async_remote_copy(
            src_ref=sb.at[g, dest, :, pl.ds(0, n)],
            dst_ref=rb.at[g, lat, :, pl.ds(0, n)],
            send_sem=z_send.at[g],
            recv_sem=z_recv.at[g],
            device_id={"lat": dest},
            device_id_type=MESH,
        )

    def z_all(g):
        n = 2 * slots(g)
        return pltpu.make_async_remote_copy(
            src_ref=sb.at[g, pl.ds(0, NLATDEV - 1), :, pl.ds(0, n)],
            dst_ref=rb.at[g, pl.ds(0, NLATDEV - 1), :, pl.ds(0, n)],
            send_sem=z_send.at[g],
            recv_sem=z_recv.at[g],
            device_id={"lat": peers[0]},
            device_id_type=MESH,
        )

    def ready_table(g):
        for par in range(2):
            c = 2 * g + par
            q = pq[par][1]
            tg[c, q] = jnp.zeros((4, LP, KP), bf16)
            if slots(g) < 4:
                for i in range(4):
                    tg[c, i, 3] = jnp.zeros((LP, KP), bf16)
            for j in range(slots(g)):
                tg[c, q, j, :LBLK, :HALF] = tv[order_of(g, par, j)]

    def t_move(c, d):
        p, q = pq[c % 2]
        to, n = lax.rem(q + d, 4), slots(c // 2)
        return pltpu.make_async_remote_copy(
            src_ref=tg.at[c, q, pl.ds(0, n)],
            dst_ref=tg.at[c, q, pl.ds(0, n)],
            send_sem=t_send.at[c],
            recv_sem=t_recv.at[c],
            device_id={"ch": ch_at(c % 2, p, to)},
            device_id_type=MESH,
        )

    def t_all(c):
        p, q = pq[c % 2]
        part = tg.at[c, pl.ds(0, 3), pl.ds(0, slots(c // 2))]
        return pltpu.make_async_remote_copy(
            src_ref=part,
            dst_ref=part,
            send_sem=t_send.at[c],
            recv_sem=t_recv.at[c],
            device_id={"ch": ch_at(c % 2, p, lax.rem(q + 1, 4))},
            device_id_type=MESH,
        )

    def p_move(c, d):
        p, q = pq[c % 2]
        return pltpu.make_async_remote_copy(
            src_ref=yp.at[c],
            dst_ref=wb.at[c, :, p],
            send_sem=p_send.at[c],
            recv_sem=p_recv.at[c],
            device_id={"ch": ch_at(c % 2, lax.rem(p + d, 4), q)},
            device_id_type=MESH,
        )

    def p_all(c):
        p, q = pq[c % 2]
        part = wb.at[c, :, pl.ds(0, 3)]
        return pltpu.make_async_remote_copy(
            src_ref=part,
            dst_ref=part,
            send_sem=p_send.at[c],
            recv_sem=p_recv.at[c],
            device_id={"ch": ch_at(c % 2, lax.rem(p + 1, 4), q)},
            device_id_type=MESH,
        )

    def o_move(c, d):
        p, q = pq[c % 2]
        to = lax.rem(q + d, 4)
        return pltpu.make_async_remote_copy(
            src_ref=ob.at[c, to],
            dst_ref=orr.at[c, q],
            send_sem=o_send.at[c],
            recv_sem=o_recv.at[c],
            device_id={"ch": ch_at(c % 2, p, to)},
            device_id_type=MESH,
        )

    def o_all(c):
        p, q = pq[c % 2]
        return pltpu.make_async_remote_copy(
            src_ref=ob.at[c, pl.ds(0, 3)],
            dst_ref=orr.at[c, pl.ds(0, 3)],
            send_sem=o_send.at[c],
            recv_sem=o_recv.at[c],
            device_id={"ch": ch_at(c % 2, p, lax.rem(q + 1, 4))},
            device_id_type=MESH,
        )

    def send_table(g):
        for c in (2 * g, 2 * g + 1):
            for d in (1, 3, 2):
                t_move(c, d).start()

    for g in range(GROUPS):
        transform(g)
        if g == 0:
            t_copy.wait()
            ready_table(0)
            pl.semaphore_wait(barrier, NLATDEV - 1 + 6)
        for peer in peers:
            z_copy(g, peer).start()
        if g < GROUPS - 1:
            if g:
                ready_table(g)
            send_table(g)

    ready_table(GROUPS - 1)

    for par in range(2):
        row = lax.broadcasted_iota(jnp.int32, (512, 512), 0)
        col = lax.broadcasted_iota(jnp.int32, (512, 512), 1)
        qq, pp = row // 128, (row // 32) % 4
        chan = ch_at(par, pp, qq)
        want = (
            ((row // 2) % 4) * 128
            + ((row // 16) % 2) * 64
            + chan * 4
            + ((row // 8) % 2) * 2
            + row % 2
        )
        pm[par] = jnp.where(want == col, 1.0, 0.0).astype(bf16)

    lane = lax.broadcasted_iota(jnp.int32, (16, 128), 1)

    def unpack(g):
        z_all(g).wait_recv()
        for b in range(4):
            acc = [[jnp.zeros((16, 128), f32) for _ in range(3)] for _ in range(2)]
            for s in range(NLATDEV // 2):
                north = rb[g, s].astype(f32).reshape(16, 128)
                other = rb[g, NLATDEV - 1 - s].astype(f32).reshape(16, 128)
                first = SLAB * s
                shift = (first - SLAB * b) % 128
                for i, val in enumerate((north + other, north - other)):
                    if shift:
                        val = pltpu.roll(val, shift, 1)
                    for t in range(first // 128, (first + SLAB - 1) // 128 + 1):
                        lo, hi = first - 128 * t, first + SLAB - 128 * t
                        inside = jnp.logical_and(lane >= lo, lane < hi)
                        acc[i][t] = jnp.where(inside, val, acc[i][t])
            for par in range(2):
                for i in range(2):
                    for t in range(3):
                        yf[par, i, b, :, 128 * t : 128 * t + 128] = acc[i][t][
                            8 * par : 8 * par + 8
                        ]
        for par in range(2):
            c = 2 * g + par
            block = yf[par].reshape(2, 32, KP).astype(bf16)
            yp[c] = block
            wb[c, :, pq[par][0]] = block
            for d in (1, 3, 2):
                p_move(c, d).start()

    rows = lax.broadcasted_iota(jnp.int32, (LP, 128), 0)
    lanes = lax.broadcasted_iota(jnp.int32, (LP, 128), 1)
    lane_slot = (lanes // 2) % 4

    def project(c):
        g, par = c // 2, c % 2
        q = pq[par][1]
        t_all(c).wait_recv()
        p_all(c).wait_recv()
        got = lax.dot_general(
            tg[c].reshape(16 * LP, KP),
            wb[c].reshape(256, KP),
            NT,
            preferred_element_type=f32,
        )
        same = rows % 2 == par
        for i in range(4):
            total = jnp.zeros((LP, 128), f32)
            for j in range(slots(g)):
                lo = (4 * i + j) * LP
                both = got[lo : lo + LP]
                val = jnp.where(same, both[:, :128], both[:, 128:])
                total = jnp.where(lane_slot == j, val, total)
            ob[c, i] = total.astype(bf16)
        orr[c, q] = ob[c, q]
        for d in (1, 3, 2):
            o_move(c, d).start()

    def finish(c):
        g, par = c // 2, c % 2
        o_all(c).wait_recv()
        full = jnp.concatenate([orr[c, i] for i in range(4)], axis=1)
        res = jnp.dot(full, pm[par], preferred_element_type=f32)
        for j in range(slots(g)):
            out_ref[order_of(g, par, j)] = res[:LBLK, 128 * j : 128 * j + 128]

    for g in range(GROUPS):
        unpack(g)
        if g == 0:
            send_table(GROUPS - 1)
        for par in range(2):
            project(2 * g + par)
        if g:
            for par in range(2):
                finish(2 * (g - 1) + par)
    for par in range(2):
        finish(2 * (GROUPS - 1) + par)

    for g in range(GROUPS):
        z_all(g).wait_send()
    for c in range(2 * GROUPS):
        t_all(c).wait_send()
        p_all(c).wait_send()
        o_all(c).wait_send()


def shards(fields, table):
    fourier = jnp.asarray(fourier_rows())
    bf16, f32 = jnp.bfloat16, jnp.float32
    dma = pltpu.SemaphoreType.DMA
    chunks = 2 * GROUPS
    return pl.pallas_call(
        kernel,
        out_shape=jax.ShapeDtypeStruct((SLAB, LBLK, 128), f32),
        in_specs=[
            pl.BlockSpec(memory_space=pl.ANY),
            pl.BlockSpec(memory_space=pl.ANY),
            pl.BlockSpec(memory_space=pl.ANY),
        ],
        out_specs=pl.BlockSpec(memory_space=pltpu.VMEM),
        scratch_shapes=[
            pltpu.VMEM((2, SLAB, 2, NLON), bf16),
            pltpu.VMEM((96, 2 * FP), f32),
            pltpu.VMEM((GROUPS, 2, NLATDEV * 8, FP), bf16),
            pltpu.VMEM((SLAB, LBLK, HALF), bf16),
            pltpu.VMEM((GROUPS, NLATDEV, 2, 8, 128), bf16),
            pltpu.VMEM((GROUPS, NLATDEV, 2, 8, 128), bf16),
            pltpu.VMEM((chunks, 4, 4, LP, KP), bf16),
            pltpu.VMEM((2, 2, 4, 8, KP), f32),
            pltpu.VMEM((chunks, 2, 32, KP), bf16),
            pltpu.VMEM((chunks, 2, 4, 32, KP), bf16),
            pltpu.VMEM((chunks, 4, LP, 128), bf16),
            pltpu.VMEM((chunks, 4, LP, 128), bf16),
            pltpu.VMEM((2, 512, 512), bf16),
            dma((3,)),
            dma((GROUPS,)),
            dma((GROUPS,)),
            dma((chunks,)),
            dma((chunks,)),
            dma((chunks,)),
            dma((chunks,)),
            dma((chunks,)),
            dma((chunks,)),
        ],
        compiler_params=pltpu.CompilerParams(
            collective_id=0, has_side_effects=True, vmem_limit_bytes=62 << 20
        ),
    )(fields, fourier, table)


def solution(mesh):
    return jax.shard_map(
        shards,
        mesh=mesh,
        in_specs=(P(None, "lat", "ch", None), P("lat", "ch", None)),
        out_specs=P("lat", "ch", None),
        check_vma=False,
    )
```

```python
import functools
import math

import numpy as np
import jax
import jax.numpy as jnp
from jax import lax
from jax.experimental import pallas as pl
from jax.experimental.pallas import tpu as pltpu
from jax.sharding import PartitionSpec as P

NLON = 1440
FOLD = NLON // 2
NZ = 16
NLATDEV = 32
SLAB = 22
LBLK = 44
HALF = 352
GROUPS = 3
LP = 48
KP = 384
FP = 768
MESH = pl.DeviceIdType.MESH
NT = (((1,), (1,)), ((), ()))


def slots(g):
    return min(4, SLAB // 2 - 4 * g)


def order_of(g, par, j):
    return 2 * (4 * g + j) + par


def fourier_rows():
    table = np.zeros((GROUPS, 2, NLATDEV, 4, 2, FP), np.float64)
    cols = np.arange(FOLD, dtype=np.int64)
    scale = 1.0 / math.sqrt(NLON)
    owners = np.arange(NLATDEV, dtype=np.int64)[:, None]
    for g in range(GROUPS):
        for par in range(2):
            for j in range(slots(g)):
                order = owners * SLAB + order_of(g, par, j)
                angle = (order * cols[None, :] % NLON) * (2.0 * math.pi / NLON)
                table[g, par, :, j, 0, :FOLD] = np.cos(angle) * scale
                table[g, par, :, j, 1, :FOLD] = -np.sin(angle) * scale
    return table.reshape(GROUPS, 2, NLATDEV * 8, FP).astype(jnp.bfloat16)


def kernel(
    x_ref, f_ref, t_ref, out_ref,
    xv, xs, fv, tv, sb, rb, tg, yf, yp, wb, ob, orr, pm,
    in_sem, z_send, z_recv, t_send, t_recv, t_last, p_send, p_recv, o_send, o_recv,
):
    f32, bf16 = jnp.float32, jnp.bfloat16
    lat = lax.axis_index("lat")
    ch = lax.axis_index("ch")
    z, core = lat // 2, lax.rem(lat, 2)
    y, x = ch // 4, lax.rem(ch, 4)

    x_copy = pltpu.make_async_copy(x_ref, xv, in_sem.at[0])
    f_copy = pltpu.make_async_copy(f_ref, fv, in_sem.at[1])
    t_copy = pltpu.make_async_copy(t_ref, tv, in_sem.at[2])
    x_copy.start()
    f_copy.start()
    t_copy.start()

    hops = [8 - (u + 1) // 2 if u % 2 else 8 + u // 2 for u in range(NZ)]
    peers = [lax.rem(z + dz, NZ) * 2 + at for dz in hops for at in (1 - core, core)][:-1]

    pq = ((x, y), (y, x))

    def ch_at(par, p, q):
        return q * 4 + p if par == 0 else p * 4 + q

    barrier = pltpu.get_barrier_semaphore()

    for peer in peers:
        pl.semaphore_signal(barrier, inc=1, device_id={"lat": peer}, device_id_type=MESH)
    for d in range(1, 4):
        for par in range(2):
            p, q = pq[par]
            pl.semaphore_signal(
                barrier, inc=1, device_id={"ch": ch_at(par, lax.rem(p + d, 4), q)}, device_id_type=MESH
            )

    dst = lax.broadcasted_iota(jnp.int32, (128, 96), 0)
    src = lax.broadcasted_iota(jnp.int32, (128, 96), 1)
    one = jnp.ones_like(dst)
    zero = jnp.zeros_like(dst)
    bc = (
        jnp.where(dst >= SLAB, one, zero)
        + jnp.where(dst >= 2 * SLAB, one, zero)
        + jnp.where(dst >= 3 * SLAB, one, zero)
    )
    k = dst - SLAB * bc
    south = jnp.where(lat >= NLATDEV // 2, 1, 0)
    k = k + south * (SLAB - 1 - 2 * k)
    want = (bc // 2) * (2 * SLAB) + 2 * k + bc % 2
    hit = jnp.logical_and(want == src, dst < 4 * SLAB)
    perm = jnp.where(hit, 1.0, 0.0).astype(bf16)
    xs[4 * SLAB :, :] = jnp.zeros((8, 2 * FP), f32)
    xs[:, NLON:] = jnp.zeros((96, 2 * FP - NLON), f32)
    x_copy.wait()
    for i in range(2 * SLAB):
        xs[2 * i : 2 * i + 2, :NLON] = xv[i // SLAB, i % SLAB].astype(f32)
    whole = xs[...]
    first = whole[:, :FP]
    second = pltpu.roll(whole, 2 * FP - FOLD, 1)[:, :FP]
    xp = [
        jnp.dot(perm, val.astype(bf16), preferred_element_type=f32).astype(bf16)
        for val in (first + second, first - second)
    ]

    f_copy.wait()

    def transform(g):
        halves = [
            lax.dot_general(fv[g, par], xp[par], NT, preferred_element_type=f32).reshape(
                NLATDEV, 8, 128
            )
            for par in range(2)
        ]
        sb[g] = jnp.stack(halves, axis=1).astype(bf16)
        rb[g, lat] = sb[g, lat]

    def z_copy(g, dest):
        n = 2 * slots(g)
        return pltpu.make_async_remote_copy(
            src_ref=sb.at[g, dest, :, pl.ds(0, n)],
            dst_ref=rb.at[g, lat, :, pl.ds(0, n)],
            send_sem=z_send.at[g],
            recv_sem=z_recv.at[g],
            device_id={"lat": dest},
            device_id_type=MESH,
        )

    def z_all(g):
        n = 2 * slots(g)
        return pltpu.make_async_remote_copy(
            src_ref=sb.at[g, pl.ds(0, NLATDEV - 1), :, pl.ds(0, n)],
            dst_ref=rb.at[g, pl.ds(0, NLATDEV - 1), :, pl.ds(0, n)],
            send_sem=z_send.at[g],
            recv_sem=z_recv.at[g],
            device_id={"lat": peers[0]},
            device_id_type=MESH,
        )

    def ready_table(g):
        for par in range(2):
            c = 2 * g + par
            q = pq[par][1]
            tg[c, q] = jnp.zeros((4, LP, KP), bf16)
            if slots(g) < 4:
                for i in range(4):
                    tg[c, i, 3] = jnp.zeros((LP, KP), bf16)
            for j in range(slots(g)):
                tg[c, q, j, :LBLK, :HALF] = tv[order_of(g, par, j)]

    def t_move(c, d):
        p, q = pq[c % 2]
        to, n = lax.rem(q + d, 4), slots(c // 2)
        return pltpu.make_async_remote_copy(
            src_ref=tg.at[c, q, pl.ds(0, n)],
            dst_ref=tg.at[c, q, pl.ds(0, n)],
            send_sem=t_send.at[c],
            recv_sem=t_recv.at[c],
            device_id={"ch": ch_at(c % 2, p, to)},
            device_id_type=MESH,
        )

    def t_pass(c, d):
        p, q = pq[c % 2]
        origin, to, n = lax.rem(q + 4 - d, 4), lax.rem(q + d, 4), slots(c // 2)
        half = pl.ds(0, 2) if d == 1 else pl.ds(2, n - 2)
        return pltpu.make_async_remote_copy(
            src_ref=tg.at[c, origin, half],
            dst_ref=tg.at[c, origin, half],
            send_sem=t_send.at[c],
            recv_sem=t_last.at[c],
            device_id={"ch": ch_at(c % 2, p, to)},
            device_id_type=MESH,
        )

    def t_all(c, blocks, recv):
        p, q = pq[c % 2]
        part = tg.at[c, pl.ds(0, blocks), pl.ds(0, slots(c // 2))]
        return pltpu.make_async_remote_copy(
            src_ref=part,
            dst_ref=part,
            send_sem=t_send.at[c],
            recv_sem=recv.at[c],
            device_id={"ch": ch_at(c % 2, p, lax.rem(q + 1, 4))},
            device_id_type=MESH,
        )

    def p_move(c, d):
        p, q = pq[c % 2]
        return pltpu.make_async_remote_copy(
            src_ref=yp.at[c],
            dst_ref=wb.at[c, :, p],
            send_sem=p_send.at[c],
            recv_sem=p_recv.at[c],
            device_id={"ch": ch_at(c % 2, lax.rem(p + d, 4), q)},
            device_id_type=MESH,
        )

    def p_all(c):
        p, q = pq[c % 2]
        part = wb.at[c, :, pl.ds(0, 3)]
        return pltpu.make_async_remote_copy(
            src_ref=part,
            dst_ref=part,
            send_sem=p_send.at[c],
            recv_sem=p_recv.at[c],
            device_id={"ch": ch_at(c % 2, lax.rem(p + 1, 4), q)},
            device_id_type=MESH,
        )

    def o_move(c, d):
        p, q = pq[c % 2]
        to = lax.rem(q + d, 4)
        return pltpu.make_async_remote_copy(
            src_ref=ob.at[c, to],
            dst_ref=orr.at[c, q],
            send_sem=o_send.at[c],
            recv_sem=o_recv.at[c],
            device_id={"ch": ch_at(c % 2, p, to)},
            device_id_type=MESH,
        )

    def o_all(c):
        p, q = pq[c % 2]
        return pltpu.make_async_remote_copy(
            src_ref=ob.at[c, pl.ds(0, 3)],
            dst_ref=orr.at[c, pl.ds(0, 3)],
            send_sem=o_send.at[c],
            recv_sem=o_recv.at[c],
            device_id={"ch": ch_at(c % 2, p, lax.rem(q + 1, 4))},
            device_id_type=MESH,
        )

    def send_table(g):
        for c in (2 * g, 2 * g + 1):
            for d in (1, 3):
                t_move(c, d).start()

    def pass_table(g):
        for c in (2 * g, 2 * g + 1):
            t_all(c, 2, t_recv).wait_recv()
            for d in (1, 3):
                t_pass(c, d).start()

    for g in range(GROUPS):
        transform(g)
        if g == 0:
            t_copy.wait()
            ready_table(0)
            pl.semaphore_wait(barrier, NLATDEV - 1 + 6)
        for peer in peers:
            z_copy(g, peer).start()
        if g < GROUPS - 1:
            if g:
                ready_table(g)
            send_table(g)

    ready_table(GROUPS - 1)

    for par in range(2):
        row = lax.broadcasted_iota(jnp.int32, (512, 512), 0)
        col = lax.broadcasted_iota(jnp.int32, (512, 512), 1)
        qq, pp = row // 128, (row // 32) % 4
        chan = ch_at(par, pp, qq)
        want = (
            ((row // 2) % 4) * 128
            + ((row // 16) % 2) * 64
            + chan * 4
            + ((row // 8) % 2) * 2
            + row % 2
        )
        pm[par] = jnp.where(want == col, 1.0, 0.0).astype(bf16)

    lane = lax.broadcasted_iota(jnp.int32, (16, 128), 1)

    def unpack(g):
        z_all(g).wait_recv()
        for b in range(4):
            acc = [[jnp.zeros((16, 128), f32) for _ in range(3)] for _ in range(2)]
            for s in range(NLATDEV // 2):
                north = rb[g, s].astype(f32).reshape(16, 128)
                other = rb[g, NLATDEV - 1 - s].astype(f32).reshape(16, 128)
                first = SLAB * s
                shift = (first - SLAB * b) % 128
                for i, val in enumerate((north + other, north - other)):
                    if shift:
                        val = pltpu.roll(val, shift, 1)
                    for t in range(first // 128, (first + SLAB - 1) // 128 + 1):
                        lo, hi = first - 128 * t, first + SLAB - 128 * t
                        inside = jnp.logical_and(lane >= lo, lane < hi)
                        acc[i][t] = jnp.where(inside, val, acc[i][t])
            for par in range(2):
                for i in range(2):
                    for t in range(3):
                        yf[par, i, b, :, 128 * t : 128 * t + 128] = acc[i][t][
                            8 * par : 8 * par + 8
                        ]
        for par in range(2):
            c = 2 * g + par
            block = yf[par].reshape(2, 32, KP).astype(bf16)
            yp[c] = block
            wb[c, :, pq[par][0]] = block
            for d in (1, 3, 2):
                p_move(c, d).start()

    rows = lax.broadcasted_iota(jnp.int32, (LP, 128), 0)
    lanes = lax.broadcasted_iota(jnp.int32, (LP, 128), 1)
    lane_slot = (lanes // 2) % 4

    def project(c):
        g, par = c // 2, c % 2
        q = pq[par][1]
        t_all(c, 1, t_last).wait_recv()
        p_all(c).wait_recv()
        got = lax.dot_general(
            tg[c].reshape(16 * LP, KP),
            wb[c].reshape(256, KP),
            NT,
            preferred_element_type=f32,
        )
        same = rows % 2 == par
        for i in range(4):
            total = jnp.zeros((LP, 128), f32)
            for j in range(slots(g)):
                lo = (4 * i + j) * LP
                both = got[lo : lo + LP]
                val = jnp.where(same, both[:, :128], both[:, 128:])
                total = jnp.where(lane_slot == j, val, total)
            ob[c, i] = total.astype(bf16)
        orr[c, q] = ob[c, q]
        for d in (1, 3, 2):
            o_move(c, d).start()

    def finish(c):
        g, par = c // 2, c % 2
        o_all(c).wait_recv()
        full = jnp.concatenate([orr[c, i] for i in range(4)], axis=1)
        res = jnp.dot(full, pm[par], preferred_element_type=f32)
        for j in range(slots(g)):
            out_ref[order_of(g, par, j)] = res[:LBLK, 128 * j : 128 * j + 128]

    def both(step, g):
        for par in range(2):
            step(2 * g + par)

    pass_table(0)
    pass_table(1)
    unpack(0)
    send_table(2)
    unpack(1)
    pass_table(2)
    both(project, 0)
    unpack(2)
    both(project, 1)
    both(finish, 0)
    both(project, 2)
    both(finish, 1)
    both(finish, 2)

    for g in range(GROUPS):
        z_all(g).wait_send()
    for c in range(2 * GROUPS):
        t_all(c, 3, t_recv).wait_send()
        p_all(c).wait_send()
        o_all(c).wait_send()


def shards(fields, table):
    fourier = jnp.asarray(fourier_rows())
    bf16, f32 = jnp.bfloat16, jnp.float32
    dma = pltpu.SemaphoreType.DMA
    chunks = 2 * GROUPS
    return pl.pallas_call(
        kernel,
        out_shape=jax.ShapeDtypeStruct((SLAB, LBLK, 128), f32),
        in_specs=[
            pl.BlockSpec(memory_space=pl.ANY),
            pl.BlockSpec(memory_space=pl.ANY),
            pl.BlockSpec(memory_space=pl.ANY),
        ],
        out_specs=pl.BlockSpec(memory_space=pltpu.VMEM),
        scratch_shapes=[
            pltpu.VMEM((2, SLAB, 2, NLON), bf16),
            pltpu.VMEM((96, 2 * FP), f32),
            pltpu.VMEM((GROUPS, 2, NLATDEV * 8, FP), bf16),
            pltpu.VMEM((SLAB, LBLK, HALF), bf16),
            pltpu.VMEM((GROUPS, NLATDEV, 2, 8, 128), bf16),
            pltpu.VMEM((GROUPS, NLATDEV, 2, 8, 128), bf16),
            pltpu.VMEM((chunks, 4, 4, LP, KP), bf16),
            pltpu.VMEM((2, 2, 4, 8, KP), f32),
            pltpu.VMEM((chunks, 2, 32, KP), bf16),
            pltpu.VMEM((chunks, 2, 4, 32, KP), bf16),
            pltpu.VMEM((chunks, 4, LP, 128), bf16),
            pltpu.VMEM((chunks, 4, LP, 128), bf16),
            pltpu.VMEM((2, 512, 512), bf16),
            dma((3,)),
            dma((GROUPS,)),
            dma((GROUPS,)),
            dma((chunks,)),
            dma((chunks,)),
            dma((chunks,)),
            dma((chunks,)),
            dma((chunks,)),
            dma((chunks,)),
            dma((chunks,)),
        ],
        compiler_params=pltpu.CompilerParams(
            collective_id=0, has_side_effects=True, vmem_limit_bytes=62 << 20
        ),
    )(fields, fourier, table)


def solution(mesh):
    return jax.shard_map(
        shards,
        mesh=mesh,
        in_specs=(P(None, "lat", "ch", None), P("lat", "ch", None)),
        out_specs=P("lat", "ch", None),
        check_vma=False,
    )
```

```python
import functools
import math

import numpy as np
import jax
import jax.numpy as jnp
from jax import lax
from jax.experimental import pallas as pl
from jax.experimental.pallas import tpu as pltpu
from jax.sharding import PartitionSpec as P

NLON = 1440
FOLD = NLON // 2
NZ = 16
NLATDEV = 32
SLAB = 22
LBLK = 44
HALF = 352
GROUPS = 3
LP = 48
KP = 384
FP = 768
MESH = pl.DeviceIdType.MESH
NT = (((1,), (1,)), ((), ()))


CHUNKS = (
    {0: 0, 1: 2, 2: 4, 3: 6},
    {0: 1, 1: 3, 2: 5, 3: 7},
    {0: 8, 1: 10, 2: 12, 3: 14},
    {0: 9, 1: 11, 2: 13, 3: 15},
    {0: 16, 1: 18, 3: 20},
    {0: 19, 1: 21, 2: 17},
)
SENT = CHUNKS[:5] + ({2: 17}, {0: 19, 1: 21})


def pieces(c):
    return ((0, 2), (3, 1)) if c == 4 else ((0, 2), (2, len(CHUNKS[c]) - 2))


def fourier_rows():
    table = np.zeros((len(SENT), NLATDEV, 4, 2, FP), np.float64)
    cols = np.arange(FOLD, dtype=np.int64)
    scale = 1.0 / math.sqrt(NLON)
    owners = np.arange(NLATDEV, dtype=np.int64)[:, None]
    for i, held in enumerate(SENT):
        for j, local in held.items():
            angle = ((owners * SLAB + local) * cols[None, :] % NLON) * (2.0 * math.pi / NLON)
            table[i, :, j, 0, :FOLD] = np.cos(angle) * scale
            table[i, :, j, 1, :FOLD] = -np.sin(angle) * scale
    return table.reshape(len(SENT), NLATDEV * 8, FP).astype(jnp.bfloat16)


def kernel(
    x_ref, f_ref, t_ref, out_ref,
    xv, xs, fv, tv, extra, sb, rb, rl, tg, yf, yp, wb, ob, orr, pm,
    in_sem, z_send, z_recv, t_send, t_recv, t_last, p_send, p_recv, o_send, o_recv,
):
    f32, bf16 = jnp.float32, jnp.bfloat16
    lat = lax.axis_index("lat")
    ch = lax.axis_index("ch")
    z, core = lat // 2, lax.rem(lat, 2)
    y, x = ch // 4, lax.rem(ch, 4)

    x_copy = pltpu.make_async_copy(x_ref, xv, in_sem.at[0])
    f_copy = pltpu.make_async_copy(f_ref, fv, in_sem.at[1])
    t_copy = pltpu.make_async_copy(t_ref, tv, in_sem.at[2])
    x_copy.start()
    f_copy.start()
    t_copy.start()

    hops = [8 - (u + 1) // 2 if u % 2 else 8 + u // 2 for u in range(NZ)]
    peers = [lax.rem(z + dz, NZ) * 2 + at for dz in hops for at in (1 - core, core)][:-1]

    pq = ((x, y), (y, x))

    def ch_at(par, p, q):
        return q * 4 + p if par == 0 else p * 4 + q

    barrier = pltpu.get_barrier_semaphore()

    for peer in peers:
        pl.semaphore_signal(barrier, inc=1, device_id={"lat": peer}, device_id_type=MESH)
    for d in range(1, 4):
        for par in range(2):
            p, q = pq[par]
            pl.semaphore_signal(
                barrier, inc=1, device_id={"ch": ch_at(par, lax.rem(p + d, 4), q)}, device_id_type=MESH
            )

    dst = lax.broadcasted_iota(jnp.int32, (128, 96), 0)
    src = lax.broadcasted_iota(jnp.int32, (128, 96), 1)
    one = jnp.ones_like(dst)
    zero = jnp.zeros_like(dst)
    bc = (
        jnp.where(dst >= SLAB, one, zero)
        + jnp.where(dst >= 2 * SLAB, one, zero)
        + jnp.where(dst >= 3 * SLAB, one, zero)
    )
    k = dst - SLAB * bc
    south = jnp.where(lat >= NLATDEV // 2, 1, 0)
    k = k + south * (SLAB - 1 - 2 * k)
    want = (bc // 2) * (2 * SLAB) + 2 * k + bc % 2
    hit = jnp.logical_and(want == src, dst < 4 * SLAB)
    perm = jnp.where(hit, 1.0, 0.0).astype(bf16)
    xs[4 * SLAB :, :] = jnp.zeros((8, 2 * FP), f32)
    xs[:, NLON:] = jnp.zeros((96, 2 * FP - NLON), f32)
    x_copy.wait()
    for i in range(2 * SLAB):
        xs[2 * i : 2 * i + 2, :NLON] = xv[i // SLAB, i % SLAB].astype(f32)
    whole = xs[...]
    first = whole[:, :FP]
    second = pltpu.roll(whole, 2 * FP - FOLD, 1)[:, :FP]
    xp = [
        jnp.dot(perm, val.astype(bf16), preferred_element_type=f32).astype(bf16)
        for val in (first + second, first - second)
    ]

    f_copy.wait()

    def rows_of(i, par):
        return lax.dot_general(fv[i], xp[par], NT, preferred_element_type=f32)

    wide = lax.broadcasted_iota(jnp.int32, (NLATDEV * 8, 128), 1)
    spare = jnp.logical_and(wide >= 4 * SLAB, wide < 5 * SLAB)

    def transform(g):
        if g == 0:
            extra[...] = rows_of(4, 0) + rows_of(5, 1)
        if g < 2:
            halves = []
            for par in range(2):
                own = rows_of(2 * g + par, par)
                moved = pltpu.roll(extra[...], (4 - (2 * g + par)) * SLAB, 1)
                halves.append(jnp.where(spare, moved, own).reshape(NLATDEV, 8, 128))
            sb[g] = jnp.stack(halves, axis=1).astype(bf16)
        else:
            sb[g, :, 0] = rows_of(6, 1).reshape(NLATDEV, 8, 128).astype(bf16)
        rb[g, lat] = sb[g, lat]

    def z_part(g):
        return (slice(None), slice(None)) if g < 2 else (0, pl.ds(0, 4))

    def z_copy(g, dest):
        return pltpu.make_async_remote_copy(
            src_ref=sb.at[(g, dest) + z_part(g)],
            dst_ref=rb.at[(g, lat) + z_part(g)],
            send_sem=z_send.at[g],
            recv_sem=z_recv.at[g],
            device_id={"lat": dest},
            device_id_type=MESH,
        )

    def z_all(g):
        every = (g, pl.ds(0, NLATDEV - 1)) + z_part(g)
        return pltpu.make_async_remote_copy(
            src_ref=sb.at[every],
            dst_ref=rb.at[every],
            send_sem=z_send.at[g],
            recv_sem=z_recv.at[g],
            device_id={"lat": peers[0]},
            device_id_type=MESH,
        )

    def ready_table(g):
        for par in range(2):
            c = 2 * g + par
            q = pq[par][1]
            tg[c, q] = jnp.zeros((4, LP, KP), bf16)
            for j in range(4):
                if j in CHUNKS[c]:
                    tg[c, q, j, :LBLK, :HALF] = tv[CHUNKS[c][j]]
                else:
                    for i in range(4):
                        tg[c, i, j] = jnp.zeros((LP, KP), bf16)

    def t_move(c, d, piece):
        p, q = pq[c % 2]
        part = tg.at[c, q, pl.ds(*piece)]
        return pltpu.make_async_remote_copy(
            src_ref=part,
            dst_ref=part,
            send_sem=t_send.at[c],
            recv_sem=t_recv.at[c],
            device_id={"ch": ch_at(c % 2, p, lax.rem(q + d, 4))},
            device_id_type=MESH,
        )

    def t_pass(c, d):
        p, q = pq[c % 2]
        origin, to = lax.rem(q + 4 - d, 4), lax.rem(q + d, 4)
        half = pl.ds(*pieces(c)[d // 2])
        return pltpu.make_async_remote_copy(
            src_ref=tg.at[c, origin, half],
            dst_ref=tg.at[c, origin, half],
            send_sem=t_send.at[c],
            recv_sem=t_last.at[c],
            device_id={"ch": ch_at(c % 2, p, to)},
            device_id_type=MESH,
        )

    def t_all(c, blocks, recv):
        p, q = pq[c % 2]
        part = tg.at[c, pl.ds(0, blocks), pl.ds(0, len(CHUNKS[c]))]
        return pltpu.make_async_remote_copy(
            src_ref=part,
            dst_ref=part,
            send_sem=t_send.at[c],
            recv_sem=recv.at[c],
            device_id={"ch": ch_at(c % 2, p, lax.rem(q + 1, 4))},
            device_id_type=MESH,
        )

    def p_move(c, d):
        p, q = pq[c % 2]
        return pltpu.make_async_remote_copy(
            src_ref=yp.at[c],
            dst_ref=wb.at[c, :, p],
            send_sem=p_send.at[c],
            recv_sem=p_recv.at[c],
            device_id={"ch": ch_at(c % 2, lax.rem(p + d, 4), q)},
            device_id_type=MESH,
        )

    def p_all(c):
        p, q = pq[c % 2]
        part = wb.at[c, :, pl.ds(0, 3)]
        return pltpu.make_async_remote_copy(
            src_ref=part,
            dst_ref=part,
            send_sem=p_send.at[c],
            recv_sem=p_recv.at[c],
            device_id={"ch": ch_at(c % 2, lax.rem(p + 1, 4), q)},
            device_id_type=MESH,
        )

    def o_move(c, d):
        p, q = pq[c % 2]
        to = lax.rem(q + d, 4)
        return pltpu.make_async_remote_copy(
            src_ref=ob.at[c, to],
            dst_ref=orr.at[c, q],
            send_sem=o_send.at[c],
            recv_sem=o_recv.at[c],
            device_id={"ch": ch_at(c % 2, p, to)},
            device_id_type=MESH,
        )

    def o_all(c):
        p, q = pq[c % 2]
        return pltpu.make_async_remote_copy(
            src_ref=ob.at[c, pl.ds(0, 3)],
            dst_ref=orr.at[c, pl.ds(0, 3)],
            send_sem=o_send.at[c],
            recv_sem=o_recv.at[c],
            device_id={"ch": ch_at(c % 2, p, lax.rem(q + 1, 4))},
            device_id_type=MESH,
        )

    def send_table(g):
        for c in (2 * g, 2 * g + 1):
            for d in (1, 3):
                for piece in pieces(c):
                    t_move(c, d, piece).start()

    def pass_table(g):
        for c in (2 * g, 2 * g + 1):
            t_all(c, 2, t_recv).wait_recv()
            for d in (1, 3):
                t_pass(c, d).start()

    for g in range(GROUPS):
        transform(g)
        if g == 0:
            t_copy.wait()
            ready_table(0)
            pl.semaphore_wait(barrier, NLATDEV - 1 + 6)
        for peer in peers:
            z_copy(g, peer).start()
        if g < GROUPS - 1:
            if g:
                ready_table(g)
            send_table(g)

    ready_table(GROUPS - 1)

    for par in range(2):
        row = lax.broadcasted_iota(jnp.int32, (512, 512), 0)
        col = lax.broadcasted_iota(jnp.int32, (512, 512), 1)
        qq, pp = row // 128, (row // 32) % 4
        chan = ch_at(par, pp, qq)
        want = (
            ((row // 2) % 4) * 128
            + ((row // 16) % 2) * 64
            + chan * 4
            + ((row // 8) % 2) * 2
            + row % 2
        )
        pm[par] = jnp.where(want == col, 1.0, 0.0).astype(bf16)

    lane = lax.broadcasted_iota(jnp.int32, (16, 128), 1)

    top = lax.broadcasted_iota(jnp.int32, (8, 128), 0) < 4

    def collect(s):
        joined = jnp.zeros((8, 128), f32)
        for b in range(4):
            moved = pltpu.roll(rb[b // 2, s, b % 2].astype(f32), 128 - (4 - b) * SLAB, 1)
            inside = jnp.logical_and(lane[:8] >= SLAB * b, lane[:8] < SLAB * (b + 1))
            joined = jnp.where(inside, moved, joined)
        rl[s, 0] = joined

    def arrived(g, s):
        return (rl[s] if g == 2 else rb[g, s].astype(f32)).reshape(16, 128)

    def unpack(g):
        if g == 2:
            for s in range(NLATDEV):
                collect(s)
        z_all(g).wait_recv()
        if g == 2:
            for s in range(NLATDEV):
                rl[s, 1] = jnp.where(top, rb[g, s, 0].astype(f32), rl[s, 0])
        for b in range(4):
            acc = [[jnp.zeros((16, 128), f32) for _ in range(3)] for _ in range(2)]
            for s in range(NLATDEV // 2):
                north = arrived(g, s)
                other = arrived(g, NLATDEV - 1 - s)
                first = SLAB * s
                shift = (first - SLAB * b) % 128
                for i, val in enumerate((north + other, north - other)):
                    if shift:
                        val = pltpu.roll(val, shift, 1)
                    for t in range(first // 128, (first + SLAB - 1) // 128 + 1):
                        lo, hi = first - 128 * t, first + SLAB - 128 * t
                        inside = jnp.logical_and(lane >= lo, lane < hi)
                        acc[i][t] = jnp.where(inside, val, acc[i][t])
            for par in range(2):
                for i in range(2):
                    for t in range(3):
                        yf[par, i, b, :, 128 * t : 128 * t + 128] = acc[i][t][
                            8 * par : 8 * par + 8
                        ]
        for par in range(2):
            c = 2 * g + par
            block = yf[par].reshape(2, 32, KP).astype(bf16)
            yp[c] = block
            wb[c, :, pq[par][0]] = block
            for d in (1, 3, 2):
                p_move(c, d).start()

    rows = lax.broadcasted_iota(jnp.int32, (LP, 128), 0)
    lanes = lax.broadcasted_iota(jnp.int32, (LP, 128), 1)
    lane_slot = (lanes // 2) % 4

    def project(c):
        par = c % 2
        q = pq[par][1]
        t_all(c, 1, t_last).wait_recv()
        p_all(c).wait_recv()
        got = lax.dot_general(
            tg[c].reshape(16 * LP, KP),
            wb[c].reshape(256, KP),
            NT,
            preferred_element_type=f32,
        )
        same = rows % 2 == par
        for i in range(4):
            total = jnp.zeros((LP, 128), f32)
            for j in CHUNKS[c]:
                lo = (4 * i + j) * LP
                both = got[lo : lo + LP]
                val = jnp.where(same, both[:, :128], both[:, 128:])
                total = jnp.where(lane_slot == j, val, total)
            ob[c, i] = total.astype(bf16)
        orr[c, q] = ob[c, q]
        for d in (1, 3, 2):
            o_move(c, d).start()

    def finish(c):
        par = c % 2
        o_all(c).wait_recv()
        full = jnp.concatenate([orr[c, i] for i in range(4)], axis=1)
        res = jnp.dot(full, pm[par], preferred_element_type=f32)
        for j, local in CHUNKS[c].items():
            out_ref[local] = res[:LBLK, 128 * j : 128 * j + 128]

    def both(step, g):
        for par in range(2):
            step(2 * g + par)

    pass_table(0)
    pass_table(1)
    unpack(0)
    send_table(2)
    unpack(1)
    unpack(2)
    pass_table(2)
    for g in range(GROUPS):
        both(project, g)
    for g in range(GROUPS):
        both(finish, g)

    for g in range(GROUPS):
        z_all(g).wait_send()
    for c in range(2 * GROUPS):
        t_all(c, 3, t_recv).wait_send()
        p_all(c).wait_send()
        o_all(c).wait_send()


def shards(fields, table):
    fourier = jnp.asarray(fourier_rows())
    bf16, f32 = jnp.bfloat16, jnp.float32
    dma = pltpu.SemaphoreType.DMA
    chunks = 2 * GROUPS
    return pl.pallas_call(
        kernel,
        out_shape=jax.ShapeDtypeStruct((SLAB, LBLK, 128), f32),
        in_specs=[
            pl.BlockSpec(memory_space=pl.ANY),
            pl.BlockSpec(memory_space=pl.ANY),
            pl.BlockSpec(memory_space=pl.ANY),
        ],
        out_specs=pl.BlockSpec(memory_space=pltpu.VMEM),
        scratch_shapes=[
            pltpu.VMEM((2, SLAB, 2, NLON), bf16),
            pltpu.VMEM((96, 2 * FP), f32),
            pltpu.VMEM((len(SENT), NLATDEV * 8, FP), bf16),
            pltpu.VMEM((SLAB, LBLK, HALF), bf16),
            pltpu.VMEM((NLATDEV * 8, 128), f32),
            pltpu.VMEM((GROUPS, NLATDEV, 2, 8, 128), bf16),
            pltpu.VMEM((GROUPS, NLATDEV, 2, 8, 128), bf16),
            pltpu.VMEM((NLATDEV, 2, 8, 128), f32),
            pltpu.VMEM((chunks, 4, 4, LP, KP), bf16),
            pltpu.VMEM((2, 2, 4, 8, KP), f32),
            pltpu.VMEM((chunks, 2, 32, KP), bf16),
            pltpu.VMEM((chunks, 2, 4, 32, KP), bf16),
            pltpu.VMEM((chunks, 4, LP, 128), bf16),
            pltpu.VMEM((chunks, 4, LP, 128), bf16),
            pltpu.VMEM((2, 512, 512), bf16),
            dma((3,)),
            dma((GROUPS,)),
            dma((GROUPS,)),
            dma((chunks,)),
            dma((chunks,)),
            dma((chunks,)),
            dma((chunks,)),
            dma((chunks,)),
            dma((chunks,)),
            dma((chunks,)),
        ],
        compiler_params=pltpu.CompilerParams(
            collective_id=0, has_side_effects=True, vmem_limit_bytes=62 << 20
        ),
    )(fields, fourier, table)


def solution(mesh):
    return jax.shard_map(
        shards,
        mesh=mesh,
        in_specs=(P(None, "lat", "ch", None), P("lat", "ch", None)),
        out_specs=P("lat", "ch", None),
        check_vma=False,
    )
```

```python
import functools
import math

import numpy as np
import jax
import jax.numpy as jnp
from jax import lax
from jax.experimental import pallas as pl
from jax.experimental.pallas import tpu as pltpu
from jax.sharding import PartitionSpec as P

NLON = 1440
FOLD = NLON // 2
NZ = 16
NLATDEV = 32
SLAB = 22
LBLK = 44
HALF = 352
GROUPS = 3
LP = 48
KP = 384
FP = 768
MESH = pl.DeviceIdType.MESH
NT = (((1,), (1,)), ((), ()))


CHUNKS = (
    {0: 0, 1: 2, 2: 4, 3: 6},
    {0: 1, 1: 3, 2: 5, 3: 7},
    {0: 8, 1: 10, 2: 12, 3: 14},
    {0: 9, 1: 11, 2: 13, 3: 15},
    {0: 16, 1: 18, 3: 20},
    {0: 19, 1: 21, 2: 17},
)
SENT = CHUNKS[:5] + ({2: 17}, {0: 19, 1: 21})


def pieces(c):
    return ((0, 2), (3, 1)) if c == 4 else ((0, 2), (2, len(CHUNKS[c]) - 2))


def fourier_rows():
    table = np.zeros((len(SENT), NLATDEV, 4, 2, FP), np.float64)
    cols = np.arange(FOLD, dtype=np.int64)
    scale = 1.0 / math.sqrt(NLON)
    owners = np.arange(NLATDEV, dtype=np.int64)[:, None]
    for i, held in enumerate(SENT):
        for j, local in held.items():
            angle = ((owners * SLAB + local) * cols[None, :] % NLON) * (2.0 * math.pi / NLON)
            table[i, :, j, 0, :FOLD] = np.cos(angle) * scale
            table[i, :, j, 1, :FOLD] = -np.sin(angle) * scale
    return table.reshape(len(SENT), NLATDEV * 8, FP).astype(jnp.bfloat16)


def kernel(
    x_ref, f_ref, t_ref, out_ref,
    xv, xs, fv, tv, extra, sb, rb, rl, tg, yf, yp, wb, ob, orr, pm,
    in_sem, z_send, z_recv, t_send, t_recv, t_last, p_send, p_recv, o_send, o_recv,
):
    f32, bf16 = jnp.float32, jnp.bfloat16
    lat = lax.axis_index("lat")
    ch = lax.axis_index("ch")
    z, core = lat // 2, lax.rem(lat, 2)
    y, x = ch // 4, lax.rem(ch, 4)

    x_copy = pltpu.make_async_copy(x_ref, xv, in_sem.at[0])
    f_copy = pltpu.make_async_copy(f_ref, fv, in_sem.at[1])
    t_copy = pltpu.make_async_copy(t_ref, tv, in_sem.at[2])
    x_copy.start()
    f_copy.start()
    t_copy.start()

    hops = [8 - (u + 1) // 2 if u % 2 else 8 + u // 2 for u in range(NZ)]
    peers = [lax.rem(z + dz, NZ) * 2 + at for dz in hops for at in (1 - core, core)][:-1]

    pq = ((x, y), (y, x))

    def ch_at(par, p, q):
        return q * 4 + p if par == 0 else p * 4 + q

    barrier = pltpu.get_barrier_semaphore()

    for peer in peers:
        pl.semaphore_signal(barrier, inc=1, device_id={"lat": peer}, device_id_type=MESH)
    for d in range(1, 4):
        for par in range(2):
            p, q = pq[par]
            pl.semaphore_signal(
                barrier, inc=1, device_id={"ch": ch_at(par, lax.rem(p + d, 4), q)}, device_id_type=MESH
            )

    dst = lax.broadcasted_iota(jnp.int32, (128, 96), 0)
    src = lax.broadcasted_iota(jnp.int32, (128, 96), 1)
    one = jnp.ones_like(dst)
    zero = jnp.zeros_like(dst)
    bc = (
        jnp.where(dst >= SLAB, one, zero)
        + jnp.where(dst >= 2 * SLAB, one, zero)
        + jnp.where(dst >= 3 * SLAB, one, zero)
    )
    k = dst - SLAB * bc
    south = jnp.where(lat >= NLATDEV // 2, 1, 0)
    k = k + south * (SLAB - 1 - 2 * k)
    want = (bc // 2) * (2 * SLAB) + 2 * k + bc % 2
    hit = jnp.logical_and(want == src, dst < 4 * SLAB)
    perm = jnp.where(hit, 1.0, 0.0).astype(bf16)
    xs[4 * SLAB :, :] = jnp.zeros((8, 2 * FP), f32)
    xs[:, NLON:] = jnp.zeros((96, 2 * FP - NLON), f32)
    x_copy.wait()
    for i in range(2 * SLAB):
        xs[2 * i : 2 * i + 2, :NLON] = xv[i // SLAB, i % SLAB].astype(f32)
    whole = xs[...]
    first = whole[:, :FP]
    second = pltpu.roll(whole, 2 * FP - FOLD, 1)[:, :FP]
    xp = [
        jnp.dot(perm, val.astype(bf16), preferred_element_type=f32).astype(bf16)
        for val in (first + second, first - second)
    ]

    f_copy.wait()

    def rows_of(i, par):
        return lax.dot_general(fv[i], xp[par], NT, preferred_element_type=f32)

    wide = lax.broadcasted_iota(jnp.int32, (NLATDEV * 8, 128), 1)
    spare = jnp.logical_and(wide >= 4 * SLAB, wide < 5 * SLAB)

    def transform(g):
        if g == 0:
            extra[...] = rows_of(4, 0) + rows_of(5, 1)
        if g < 2:
            halves = []
            for par in range(2):
                own = rows_of(2 * g + par, par)
                moved = pltpu.roll(extra[...], (4 - (2 * g + par)) * SLAB, 1)
                halves.append(jnp.where(spare, moved, own).reshape(NLATDEV, 8, 128))
            sb[g] = jnp.stack(halves, axis=1).astype(bf16)
        else:
            sb[g, :, 0] = rows_of(6, 1).reshape(NLATDEV, 8, 128).astype(bf16)
        rb[g, lat] = sb[g, lat]

    def z_part(g):
        return (slice(None), slice(None)) if g < 2 else (0, pl.ds(0, 4))

    def z_copy(g, dest):
        return pltpu.make_async_remote_copy(
            src_ref=sb.at[(g, dest) + z_part(g)],
            dst_ref=rb.at[(g, lat) + z_part(g)],
            send_sem=z_send.at[g],
            recv_sem=z_recv.at[g],
            device_id={"lat": dest},
            device_id_type=MESH,
        )

    def z_all(g):
        every = (g, pl.ds(0, NLATDEV - 1)) + z_part(g)
        return pltpu.make_async_remote_copy(
            src_ref=sb.at[every],
            dst_ref=rb.at[every],
            send_sem=z_send.at[g],
            recv_sem=z_recv.at[g],
            device_id={"lat": peers[0]},
            device_id_type=MESH,
        )

    def ready_table(g):
        for par in range(2):
            c = 2 * g + par
            q = pq[par][1]
            tg[c, q] = jnp.zeros((4, LP, KP), bf16)
            for j in range(4):
                if j in CHUNKS[c]:
                    tg[c, q, j, :LBLK, :HALF] = tv[CHUNKS[c][j]]
                else:
                    for i in range(4):
                        tg[c, i, j] = jnp.zeros((LP, KP), bf16)

    def t_move(c, d, piece):
        p, q = pq[c % 2]
        part = tg.at[c, q, pl.ds(*piece)]
        return pltpu.make_async_remote_copy(
            src_ref=part,
            dst_ref=part,
            send_sem=t_send.at[c],
            recv_sem=t_recv.at[c],
            device_id={"ch": ch_at(c % 2, p, lax.rem(q + d, 4))},
            device_id_type=MESH,
        )

    def t_pass(c, d):
        p, q = pq[c % 2]
        origin, to = lax.rem(q + 4 - d, 4), lax.rem(q + d, 4)
        half = pl.ds(*pieces(c)[d // 2])
        return pltpu.make_async_remote_copy(
            src_ref=tg.at[c, origin, half],
            dst_ref=tg.at[c, origin, half],
            send_sem=t_send.at[c],
            recv_sem=t_last.at[c],
            device_id={"ch": ch_at(c % 2, p, to)},
            device_id_type=MESH,
        )

    def t_all(c, blocks, recv):
        p, q = pq[c % 2]
        part = tg.at[c, pl.ds(0, blocks), pl.ds(0, len(CHUNKS[c]))]
        return pltpu.make_async_remote_copy(
            src_ref=part,
            dst_ref=part,
            send_sem=t_send.at[c],
            recv_sem=recv.at[c],
            device_id={"ch": ch_at(c % 2, p, lax.rem(q + 1, 4))},
            device_id_type=MESH,
        )

    def p_move(c, d):
        p, q = pq[c % 2]
        return pltpu.make_async_remote_copy(
            src_ref=yp.at[c],
            dst_ref=wb.at[c, :, p],
            send_sem=p_send.at[c],
            recv_sem=p_recv.at[c],
            device_id={"ch": ch_at(c % 2, lax.rem(p + d, 4), q)},
            device_id_type=MESH,
        )

    def p_all(c):
        p, q = pq[c % 2]
        part = wb.at[c, :, pl.ds(0, 3)]
        return pltpu.make_async_remote_copy(
            src_ref=part,
            dst_ref=part,
            send_sem=p_send.at[c],
            recv_sem=p_recv.at[c],
            device_id={"ch": ch_at(c % 2, lax.rem(p + 1, 4), q)},
            device_id_type=MESH,
        )

    def o_move(c, d):
        p, q = pq[c % 2]
        to = lax.rem(q + d, 4)
        return pltpu.make_async_remote_copy(
            src_ref=ob.at[c, to],
            dst_ref=orr.at[c, q],
            send_sem=o_send.at[c],
            recv_sem=o_recv.at[c],
            device_id={"ch": ch_at(c % 2, p, to)},
            device_id_type=MESH,
        )

    def o_all(c):
        p, q = pq[c % 2]
        return pltpu.make_async_remote_copy(
            src_ref=ob.at[c, pl.ds(0, 3)],
            dst_ref=orr.at[c, pl.ds(0, 3)],
            send_sem=o_send.at[c],
            recv_sem=o_recv.at[c],
            device_id={"ch": ch_at(c % 2, p, lax.rem(q + 1, 4))},
            device_id_type=MESH,
        )

    def send_table(g):
        for c in (2 * g, 2 * g + 1):
            for d in (1, 3):
                for piece in pieces(c):
                    t_move(c, d, piece).start()

    def pass_table(g):
        for c in (2 * g, 2 * g + 1):
            t_all(c, 2, t_recv).wait_recv()
            for d in (1, 3):
                t_pass(c, d).start()

    for g in range(GROUPS):
        transform(g)
        if g == 0:
            t_copy.wait()
            ready_table(0)
            pl.semaphore_wait(barrier, NLATDEV - 1 + 6)
        for peer in peers:
            z_copy(g, peer).start()
        if g:
            ready_table(g)
        send_table(g)

    for par in range(2):
        row = lax.broadcasted_iota(jnp.int32, (512, 512), 0)
        col = lax.broadcasted_iota(jnp.int32, (512, 512), 1)
        qq, pp = row // 128, (row // 32) % 4
        chan = ch_at(par, pp, qq)
        want = (
            ((row // 2) % 4) * 128
            + ((row // 16) % 2) * 64
            + chan * 4
            + ((row // 8) % 2) * 2
            + row % 2
        )
        pm[par] = jnp.where(want == col, 1.0, 0.0).astype(bf16)

    lane = lax.broadcasted_iota(jnp.int32, (16, 128), 1)

    top = lax.broadcasted_iota(jnp.int32, (8, 128), 0) < 4

    def collect(s):
        joined = jnp.zeros((8, 128), f32)
        for b in range(4):
            moved = pltpu.roll(rb[b // 2, s, b % 2].astype(f32), 128 - (4 - b) * SLAB, 1)
            inside = jnp.logical_and(lane[:8] >= SLAB * b, lane[:8] < SLAB * (b + 1))
            joined = jnp.where(inside, moved, joined)
        rl[s, 0] = joined

    def arrived(g, s):
        return (rl[s] if g == 2 else rb[g, s].astype(f32)).reshape(16, 128)

    def unpack(g):
        if g == 2:
            for s in range(NLATDEV):
                collect(s)
        z_all(g).wait_recv()
        if g == 2:
            for s in range(NLATDEV):
                rl[s, 1] = jnp.where(top, rb[g, s, 0].astype(f32), rl[s, 0])
        for b in range(4):
            acc = [[jnp.zeros((16, 128), f32) for _ in range(3)] for _ in range(2)]
            for s in range(NLATDEV // 2):
                north = arrived(g, s)
                other = arrived(g, NLATDEV - 1 - s)
                first = SLAB * s
                shift = (first - SLAB * b) % 128
                for i, val in enumerate((north + other, north - other)):
                    if shift:
                        val = pltpu.roll(val, shift, 1)
                    for t in range(first // 128, (first + SLAB - 1) // 128 + 1):
                        lo, hi = first - 128 * t, first + SLAB - 128 * t
                        inside = jnp.logical_and(lane >= lo, lane < hi)
                        acc[i][t] = jnp.where(inside, val, acc[i][t])
            for par in range(2):
                for i in range(2):
                    for t in range(3):
                        yf[par, i, b, :, 128 * t : 128 * t + 128] = acc[i][t][
                            8 * par : 8 * par + 8
                        ]
        for par in range(2):
            c = 2 * g + par
            block = yf[par].reshape(2, 32, KP).astype(bf16)
            yp[c] = block
            wb[c, :, pq[par][0]] = block
            for d in (1, 3, 2):
                p_move(c, d).start()

    rows = lax.broadcasted_iota(jnp.int32, (LP, 128), 0)
    lanes = lax.broadcasted_iota(jnp.int32, (LP, 128), 1)
    lane_slot = (lanes // 2) % 4

    def project(c):
        par = c % 2
        q = pq[par][1]
        t_all(c, 1, t_last).wait_recv()
        p_all(c).wait_recv()
        got = lax.dot_general(
            tg[c].reshape(16 * LP, KP),
            wb[c].reshape(256, KP),
            NT,
            preferred_element_type=f32,
        )
        same = rows % 2 == par
        for i in range(4):
            total = jnp.zeros((LP, 128), f32)
            for j in CHUNKS[c]:
                lo = (4 * i + j) * LP
                both = got[lo : lo + LP]
                val = jnp.where(same, both[:, :128], both[:, 128:])
                total = jnp.where(lane_slot == j, val, total)
            ob[c, i] = total.astype(bf16)
        orr[c, q] = ob[c, q]
        for d in (1, 3, 2):
            o_move(c, d).start()

    def finish(c):
        par = c % 2
        o_all(c).wait_recv()
        full = jnp.concatenate([orr[c, i] for i in range(4)], axis=1)
        res = jnp.dot(full, pm[par], preferred_element_type=f32)
        for j, local in CHUNKS[c].items():
            out_ref[local] = res[:LBLK, 128 * j : 128 * j + 128]

    def both(step, g):
        for par in range(2):
            step(2 * g + par)

    pass_table(0)
    pass_table(1)
    unpack(0)
    pass_table(2)
    unpack(1)
    unpack(2)
    for g in range(GROUPS):
        both(project, g)
    for g in range(GROUPS):
        both(finish, g)

    for g in range(GROUPS):
        z_all(g).wait_send()
    for c in range(2 * GROUPS):
        t_all(c, 3, t_recv).wait_send()
        p_all(c).wait_send()
        o_all(c).wait_send()


def shards(fields, table):
    fourier = jnp.asarray(fourier_rows())
    bf16, f32 = jnp.bfloat16, jnp.float32
    dma = pltpu.SemaphoreType.DMA
    chunks = 2 * GROUPS
    return pl.pallas_call(
        kernel,
        out_shape=jax.ShapeDtypeStruct((SLAB, LBLK, 128), f32),
        in_specs=[
            pl.BlockSpec(memory_space=pl.ANY),
            pl.BlockSpec(memory_space=pl.ANY),
            pl.BlockSpec(memory_space=pl.ANY),
        ],
        out_specs=pl.BlockSpec(memory_space=pltpu.VMEM),
        scratch_shapes=[
            pltpu.VMEM((2, SLAB, 2, NLON), bf16),
            pltpu.VMEM((96, 2 * FP), f32),
            pltpu.VMEM((len(SENT), NLATDEV * 8, FP), bf16),
            pltpu.VMEM((SLAB, LBLK, HALF), bf16),
            pltpu.VMEM((NLATDEV * 8, 128), f32),
            pltpu.VMEM((GROUPS, NLATDEV, 2, 8, 128), bf16),
            pltpu.VMEM((GROUPS, NLATDEV, 2, 8, 128), bf16),
            pltpu.VMEM((NLATDEV, 2, 8, 128), f32),
            pltpu.VMEM((chunks, 4, 4, LP, KP), bf16),
            pltpu.VMEM((2, 2, 4, 8, KP), f32),
            pltpu.VMEM((chunks, 2, 32, KP), bf16),
            pltpu.VMEM((chunks, 2, 4, 32, KP), bf16),
            pltpu.VMEM((chunks, 4, LP, 128), bf16),
            pltpu.VMEM((chunks, 4, LP, 128), bf16),
            pltpu.VMEM((2, 512, 512), bf16),
            dma((3,)),
            dma((GROUPS,)),
            dma((GROUPS,)),
            dma((chunks,)),
            dma((chunks,)),
            dma((chunks,)),
            dma((chunks,)),
            dma((chunks,)),
            dma((chunks,)),
            dma((chunks,)),
        ],
        compiler_params=pltpu.CompilerParams(
            collective_id=0, has_side_effects=True, vmem_limit_bytes=62 << 20
        ),
    )(fields, fourier, table)


def solution(mesh):
    return jax.shard_map(
        shards,
        mesh=mesh,
        in_specs=(P(None, "lat", "ch", None), P("lat", "ch", None)),
        out_specs=P("lat", "ch", None),
        check_vma=False,
    )
```

```python
import functools
import math

import numpy as np
import jax
import jax.numpy as jnp
from jax import lax
from jax.experimental import pallas as pl
from jax.experimental.pallas import tpu as pltpu
from jax.sharding import PartitionSpec as P

NLON = 1440
FOLD = NLON // 2
NZ = 16
NLATDEV = 32
SLAB = 22
LBLK = 44
HALF = 352
GROUPS = 3
LP = 48
KP = 384
FP = 768
MESH = pl.DeviceIdType.MESH
NT = (((1,), (1,)), ((), ()))


CHUNKS = (
    {0: 0, 1: 2, 2: 4, 3: 6},
    {0: 1, 1: 3, 2: 5, 3: 7},
    {0: 8, 1: 10, 2: 12, 3: 14},
    {0: 9, 1: 11, 2: 13, 3: 15},
    {0: 16, 1: 18, 3: 20},
    {0: 19, 1: 21, 2: 17},
)
SENT = CHUNKS[:5] + ({2: 17}, {0: 19, 1: 21})


def pieces(c):
    return ((0, 2), (3, 1)) if c == 4 else ((0, 2), (2, len(CHUNKS[c]) - 2))


def fourier_rows():
    table = np.zeros((len(SENT), NLATDEV, 4, 2, FP), np.float64)
    cols = np.arange(FOLD, dtype=np.int64)
    scale = 1.0 / math.sqrt(NLON)
    owners = np.arange(NLATDEV, dtype=np.int64)[:, None]
    for i, held in enumerate(SENT):
        for j, local in held.items():
            angle = ((owners * SLAB + local) * cols[None, :] % NLON) * (2.0 * math.pi / NLON)
            table[i, :, j, 0, :FOLD] = np.cos(angle) * scale
            table[i, :, j, 1, :FOLD] = -np.sin(angle) * scale
    return table.reshape(len(SENT), NLATDEV * 8, FP).astype(jnp.bfloat16)


def kernel(
    x_ref, f_ref, t_ref, out_ref,
    xv, xs, fv, tv, extra, sb, rb, rl, tg, yf, yp, wb, ob, orr, pm, ov,
    in_sem, z_send, z_recv, t_send, t_recv, t_last, p_send, p_recv, o_send, o_recv, out_sem,
):
    f32, bf16 = jnp.float32, jnp.bfloat16
    lat = lax.axis_index("lat")
    ch = lax.axis_index("ch")
    z, core = lat // 2, lax.rem(lat, 2)
    y, x = ch // 4, lax.rem(ch, 4)

    x_copy = pltpu.make_async_copy(x_ref, xv, in_sem.at[0])
    f_copy = pltpu.make_async_copy(f_ref, fv, in_sem.at[1])
    t_copy = pltpu.make_async_copy(t_ref, tv, in_sem.at[2])
    x_copy.start()
    f_copy.start()
    t_copy.start()

    hops = [8 - (u + 1) // 2 if u % 2 else 8 + u // 2 for u in range(NZ)]
    peers = [lax.rem(z + dz, NZ) * 2 + at for dz in hops for at in (1 - core, core)][:-1]

    pq = ((x, y), (y, x))

    def ch_at(par, p, q):
        return q * 4 + p if par == 0 else p * 4 + q

    barrier = pltpu.get_barrier_semaphore()

    for peer in peers:
        pl.semaphore_signal(barrier, inc=1, device_id={"lat": peer}, device_id_type=MESH)
    for d in range(1, 4):
        for par in range(2):
            p, q = pq[par]
            pl.semaphore_signal(
                barrier, inc=1, device_id={"ch": ch_at(par, lax.rem(p + d, 4), q)}, device_id_type=MESH
            )

    dst = lax.broadcasted_iota(jnp.int32, (128, 96), 0)
    src = lax.broadcasted_iota(jnp.int32, (128, 96), 1)
    one = jnp.ones_like(dst)
    zero = jnp.zeros_like(dst)
    bc = (
        jnp.where(dst >= SLAB, one, zero)
        + jnp.where(dst >= 2 * SLAB, one, zero)
        + jnp.where(dst >= 3 * SLAB, one, zero)
    )
    k = dst - SLAB * bc
    south = jnp.where(lat >= NLATDEV // 2, 1, 0)
    k = k + south * (SLAB - 1 - 2 * k)
    want = (bc // 2) * (2 * SLAB) + 2 * k + bc % 2
    hit = jnp.logical_and(want == src, dst < 4 * SLAB)
    perm = jnp.where(hit, 1.0, 0.0).astype(bf16)
    xs[4 * SLAB :, :] = jnp.zeros((8, 2 * FP), f32)
    xs[:, NLON:] = jnp.zeros((96, 2 * FP - NLON), f32)
    x_copy.wait()
    for i in range(2 * SLAB):
        xs[2 * i : 2 * i + 2, :NLON] = xv[i // SLAB, i % SLAB].astype(f32)
    whole = xs[...]
    first = whole[:, :FP]
    second = pltpu.roll(whole, 2 * FP - FOLD, 1)[:, :FP]
    xp = [
        jnp.dot(perm, val.astype(bf16), preferred_element_type=f32).astype(bf16)
        for val in (first + second, first - second)
    ]

    f_copy.wait()

    def rows_of(i, par):
        return lax.dot_general(fv[i], xp[par], NT, preferred_element_type=f32)

    wide = lax.broadcasted_iota(jnp.int32, (NLATDEV * 8, 128), 1)
    spare = jnp.logical_and(wide >= 4 * SLAB, wide < 5 * SLAB)

    def transform(g):
        if g == 0:
            extra[...] = rows_of(4, 0) + rows_of(5, 1)
        if g < 2:
            halves = []
            for par in range(2):
                own = rows_of(2 * g + par, par)
                moved = pltpu.roll(extra[...], (4 - (2 * g + par)) * SLAB, 1)
                halves.append(jnp.where(spare, moved, own).reshape(NLATDEV, 8, 128))
            sb[g] = jnp.stack(halves, axis=1).astype(bf16)
        else:
            sb[g, :, 0] = rows_of(6, 1).reshape(NLATDEV, 8, 128).astype(bf16)
        rb[g, lat] = sb[g, lat]

    def z_part(g):
        return (slice(None), slice(None)) if g < 2 else (0, pl.ds(0, 4))

    def z_copy(g, dest):
        return pltpu.make_async_remote_copy(
            src_ref=sb.at[(g, dest) + z_part(g)],
            dst_ref=rb.at[(g, lat) + z_part(g)],
            send_sem=z_send.at[g],
            recv_sem=z_recv.at[g],
            device_id={"lat": dest},
            device_id_type=MESH,
        )

    def z_all(g):
        every = (g, pl.ds(0, NLATDEV - 1)) + z_part(g)
        return pltpu.make_async_remote_copy(
            src_ref=sb.at[every],
            dst_ref=rb.at[every],
            send_sem=z_send.at[g],
            recv_sem=z_recv.at[g],
            device_id={"lat": peers[0]},
            device_id_type=MESH,
        )

    def ready_table(g):
        for par in range(2):
            c = 2 * g + par
            q = pq[par][1]
            tg[c, q] = jnp.zeros((4, LP, KP), bf16)
            for j in range(4):
                if j in CHUNKS[c]:
                    tg[c, q, j, :LBLK, :HALF] = tv[CHUNKS[c][j]]
                else:
                    for i in range(4):
                        tg[c, i, j] = jnp.zeros((LP, KP), bf16)

    def t_move(c, d, piece):
        p, q = pq[c % 2]
        part = tg.at[c, q, pl.ds(*piece)]
        return pltpu.make_async_remote_copy(
            src_ref=part,
            dst_ref=part,
            send_sem=t_send.at[c],
            recv_sem=t_recv.at[c],
            device_id={"ch": ch_at(c % 2, p, lax.rem(q + d, 4))},
            device_id_type=MESH,
        )

    def t_pass(c, d):
        p, q = pq[c % 2]
        origin, to = lax.rem(q + 4 - d, 4), lax.rem(q + d, 4)
        half = pl.ds(*pieces(c)[d // 2])
        return pltpu.make_async_remote_copy(
            src_ref=tg.at[c, origin, half],
            dst_ref=tg.at[c, origin, half],
            send_sem=t_send.at[c],
            recv_sem=t_last.at[c],
            device_id={"ch": ch_at(c % 2, p, to)},
            device_id_type=MESH,
        )

    def t_all(c, blocks, recv):
        p, q = pq[c % 2]
        part = tg.at[c, pl.ds(0, blocks), pl.ds(0, len(CHUNKS[c]))]
        return pltpu.make_async_remote_copy(
            src_ref=part,
            dst_ref=part,
            send_sem=t_send.at[c],
            recv_sem=recv.at[c],
            device_id={"ch": ch_at(c % 2, p, lax.rem(q + 1, 4))},
            device_id_type=MESH,
        )

    def p_move(c, d):
        p, q = pq[c % 2]
        return pltpu.make_async_remote_copy(
            src_ref=yp.at[c],
            dst_ref=wb.at[c, :, p],
            send_sem=p_send.at[c],
            recv_sem=p_recv.at[c],
            device_id={"ch": ch_at(c % 2, lax.rem(p + d, 4), q)},
            device_id_type=MESH,
        )

    def p_all(c):
        p, q = pq[c % 2]
        part = wb.at[c, :, pl.ds(0, 3)]
        return pltpu.make_async_remote_copy(
            src_ref=part,
            dst_ref=part,
            send_sem=p_send.at[c],
            recv_sem=p_recv.at[c],
            device_id={"ch": ch_at(c % 2, lax.rem(p + 1, 4), q)},
            device_id_type=MESH,
        )

    def o_move(c, d):
        p, q = pq[c % 2]
        to = lax.rem(q + d, 4)
        return pltpu.make_async_remote_copy(
            src_ref=ob.at[c, to],
            dst_ref=orr.at[c, q],
            send_sem=o_send.at[c],
            recv_sem=o_recv.at[c],
            device_id={"ch": ch_at(c % 2, p, to)},
            device_id_type=MESH,
        )

    def o_all(c):
        p, q = pq[c % 2]
        return pltpu.make_async_remote_copy(
            src_ref=ob.at[c, pl.ds(0, 3)],
            dst_ref=orr.at[c, pl.ds(0, 3)],
            send_sem=o_send.at[c],
            recv_sem=o_recv.at[c],
            device_id={"ch": ch_at(c % 2, p, lax.rem(q + 1, 4))},
            device_id_type=MESH,
        )

    def send_table(g):
        for c in (2 * g, 2 * g + 1):
            for d in (1, 3):
                for piece in pieces(c):
                    t_move(c, d, piece).start()

    def pass_table(g):
        for c in (2 * g, 2 * g + 1):
            t_all(c, 2, t_recv).wait_recv()
            for d in (1, 3):
                t_pass(c, d).start()

    for g in range(GROUPS):
        transform(g)
        if g == 0:
            t_copy.wait()
            ready_table(0)
            pl.semaphore_wait(barrier, NLATDEV - 1 + 6)
        for peer in peers:
            z_copy(g, peer).start()
        if g:
            ready_table(g)
        send_table(g)

    for par in range(2):
        row = lax.broadcasted_iota(jnp.int32, (512, 512), 0)
        col = lax.broadcasted_iota(jnp.int32, (512, 512), 1)
        qq, pp = row // 128, (row // 32) % 4
        chan = ch_at(par, pp, qq)
        want = (
            ((row // 2) % 4) * 128
            + ((row // 16) % 2) * 64
            + chan * 4
            + ((row // 8) % 2) * 2
            + row % 2
        )
        pm[par] = jnp.where(want == col, 1.0, 0.0).astype(bf16)

    lane = lax.broadcasted_iota(jnp.int32, (16, 128), 1)

    top = lax.broadcasted_iota(jnp.int32, (8, 128), 0) < 4

    def collect(s):
        joined = jnp.zeros((8, 128), f32)
        for b in range(4):
            moved = pltpu.roll(rb[b // 2, s, b % 2].astype(f32), 128 - (4 - b) * SLAB, 1)
            inside = jnp.logical_and(lane[:8] >= SLAB * b, lane[:8] < SLAB * (b + 1))
            joined = jnp.where(inside, moved, joined)
        rl[s, 0] = joined

    def arrived(g, s):
        return (rl[s] if g == 2 else rb[g, s].astype(f32)).reshape(16, 128)

    def unpack(g):
        if g == 2:
            for s in range(NLATDEV):
                collect(s)
        z_all(g).wait_recv()
        if g == 2:
            for s in range(NLATDEV):
                rl[s, 1] = jnp.where(top, rb[g, s, 0].astype(f32), rl[s, 0])
        for b in range(4):
            acc = [[jnp.zeros((16, 128), f32) for _ in range(3)] for _ in range(2)]
            for s in range(NLATDEV // 2):
                north = arrived(g, s)
                other = arrived(g, NLATDEV - 1 - s)
                first = SLAB * s
                shift = (first - SLAB * b) % 128
                for i, val in enumerate((north + other, north - other)):
                    if shift:
                        val = pltpu.roll(val, shift, 1)
                    for t in range(first // 128, (first + SLAB - 1) // 128 + 1):
                        lo, hi = first - 128 * t, first + SLAB - 128 * t
                        inside = jnp.logical_and(lane >= lo, lane < hi)
                        acc[i][t] = jnp.where(inside, val, acc[i][t])
            for par in range(2):
                for i in range(2):
                    for t in range(3):
                        yf[par, i, b, :, 128 * t : 128 * t + 128] = acc[i][t][
                            8 * par : 8 * par + 8
                        ]
        for par in range(2):
            c = 2 * g + par
            block = yf[par].reshape(2, 32, KP).astype(bf16)
            yp[c] = block
            wb[c, :, pq[par][0]] = block
            for d in (1, 3, 2):
                p_move(c, d).start()

    rows = lax.broadcasted_iota(jnp.int32, (LP, 128), 0)
    lanes = lax.broadcasted_iota(jnp.int32, (LP, 128), 1)
    lane_slot = (lanes // 2) % 4

    def project(c):
        par = c % 2
        q = pq[par][1]
        t_all(c, 1, t_last).wait_recv()
        p_all(c).wait_recv()
        got = lax.dot_general(
            tg[c].reshape(16 * LP, KP),
            wb[c].reshape(256, KP),
            NT,
            preferred_element_type=f32,
        )
        same = rows % 2 == par
        for i in range(4):
            total = jnp.zeros((LP, 128), f32)
            for j in CHUNKS[c]:
                lo = (4 * i + j) * LP
                both = got[lo : lo + LP]
                val = jnp.where(same, both[:, :128], both[:, 128:])
                total = jnp.where(lane_slot == j, val, total)
            ob[c, i] = total.astype(bf16)
        orr[c, q] = ob[c, q]
        for d in (1, 3, 2):
            o_move(c, d).start()

    def finish(c):
        par = c % 2
        o_all(c).wait_recv()
        full = jnp.concatenate([orr[c, i] for i in range(4)], axis=1)
        res = jnp.dot(full, pm[par], preferred_element_type=f32)
        for j, local in CHUNKS[c].items():
            ov[local] = res[:LBLK, 128 * j : 128 * j + 128]
            pltpu.make_async_copy(ov.at[local], out_ref.at[local], out_sem.at[c]).start()

    def both(step, g):
        for par in range(2):
            step(2 * g + par)

    pass_table(0)
    pass_table(1)
    unpack(0)
    pass_table(2)
    unpack(1)
    unpack(2)
    for g in range(GROUPS):
        both(project, g)
    for g in range(GROUPS):
        z_all(g).wait_send()
    for c in range(2 * GROUPS):
        t_all(c, 3, t_recv).wait_send()
    for g in range(GROUPS):
        both(finish, g)
    for c in range(2 * GROUPS):
        p_all(c).wait_send()
        o_all(c).wait_send()
        whole = pl.ds(0, len(CHUNKS[c]))
        pltpu.make_async_copy(ov.at[whole], out_ref.at[whole], out_sem.at[c]).wait()


def shards(fields, table):
    fourier = jnp.asarray(fourier_rows())
    bf16, f32 = jnp.bfloat16, jnp.float32
    dma = pltpu.SemaphoreType.DMA
    chunks = 2 * GROUPS
    return pl.pallas_call(
        kernel,
        out_shape=jax.ShapeDtypeStruct((SLAB, LBLK, 128), f32),
        in_specs=[
            pl.BlockSpec(memory_space=pl.ANY),
            pl.BlockSpec(memory_space=pl.ANY),
            pl.BlockSpec(memory_space=pl.ANY),
        ],
        out_specs=pl.BlockSpec(memory_space=pl.ANY),
        scratch_shapes=[
            pltpu.VMEM((2, SLAB, 2, NLON), bf16),
            pltpu.VMEM((96, 2 * FP), f32),
            pltpu.VMEM((len(SENT), NLATDEV * 8, FP), bf16),
            pltpu.VMEM((SLAB, LBLK, HALF), bf16),
            pltpu.VMEM((NLATDEV * 8, 128), f32),
            pltpu.VMEM((GROUPS, NLATDEV, 2, 8, 128), bf16),
            pltpu.VMEM((GROUPS, NLATDEV, 2, 8, 128), bf16),
            pltpu.VMEM((NLATDEV, 2, 8, 128), f32),
            pltpu.VMEM((chunks, 4, 4, LP, KP), bf16),
            pltpu.VMEM((2, 2, 4, 8, KP), f32),
            pltpu.VMEM((chunks, 2, 32, KP), bf16),
            pltpu.VMEM((chunks, 2, 4, 32, KP), bf16),
            pltpu.VMEM((chunks, 4, LP, 128), bf16),
            pltpu.VMEM((chunks, 4, LP, 128), bf16),
            pltpu.VMEM((2, 512, 512), bf16),
            pltpu.VMEM((SLAB, LBLK, 128), f32),
            dma((3,)),
            dma((GROUPS,)),
            dma((GROUPS,)),
            dma((chunks,)),
            dma((chunks,)),
            dma((chunks,)),
            dma((chunks,)),
            dma((chunks,)),
            dma((chunks,)),
            dma((chunks,)),
            dma((chunks,)),
        ],
        compiler_params=pltpu.CompilerParams(
            collective_id=0, has_side_effects=True, vmem_limit_bytes=62 << 20
        ),
    )(fields, fourier, table)


def solution(mesh):
    return jax.shard_map(
        shards,
        mesh=mesh,
        in_specs=(P(None, "lat", "ch", None), P("lat", "ch", None)),
        out_specs=P("lat", "ch", None),
        check_vma=False,
    )
```

```python
import functools
import math

import numpy as np
import jax
import jax.numpy as jnp
from jax import lax
from jax.experimental import pallas as pl
from jax.experimental.pallas import tpu as pltpu
from jax.sharding import PartitionSpec as P

NLON = 1440
FOLD = NLON // 2
NZ = 16
NLATDEV = 32
SLAB = 22
LBLK = 44
HALF = 352
GROUPS = 3
LP = 48
KP = 384
FP = 768
MESH = pl.DeviceIdType.MESH
NT = (((1,), (1,)), ((), ()))


CHUNKS = (
    {0: 0, 1: 2, 2: 4, 3: 6},
    {0: 1, 1: 3, 2: 5, 3: 7},
    {0: 8, 1: 10, 2: 12, 3: 14},
    {0: 9, 1: 11, 2: 13, 3: 15},
    {0: 16, 1: 18, 3: 20},
    {0: 19, 1: 21, 2: 17},
)
SENT = CHUNKS[:5] + ({2: 17}, {0: 19, 1: 21})


def pieces(c):
    return ((0, 2), (3, 1)) if c == 4 else ((0, 2), (2, len(CHUNKS[c]) - 2))


def fourier_rows():
    table = np.zeros((len(SENT), NLATDEV, 4, 2, FP), np.float64)
    cols = np.arange(FOLD, dtype=np.int64)
    scale = 1.0 / math.sqrt(NLON)
    owners = np.arange(NLATDEV, dtype=np.int64)[:, None]
    for i, held in enumerate(SENT):
        for j, local in held.items():
            angle = ((owners * SLAB + local) * cols[None, :] % NLON) * (2.0 * math.pi / NLON)
            table[i, :, j, 0, :FOLD] = np.cos(angle) * scale
            table[i, :, j, 1, :FOLD] = -np.sin(angle) * scale
    return table.reshape(len(SENT), NLATDEV * 8, FP).astype(jnp.bfloat16)


def kernel(
    x_ref, f_ref, t_ref, out_ref,
    xv, xs, fv, tv, extra, sb, rb, rl, tg, yf, yp, wb, ob, orr, pm, ov,
    in_sem, z_send, z_recv, t_send, t_recv, t_last, p_send, p_recv, o_send, o_recv, out_sem,
):
    f32, bf16 = jnp.float32, jnp.bfloat16
    lat = lax.axis_index("lat")
    ch = lax.axis_index("ch")
    z, core = lat // 2, lax.rem(lat, 2)
    y, x = ch // 4, lax.rem(ch, 4)

    x_copy = pltpu.make_async_copy(x_ref, xv, in_sem.at[0])
    f_copy = pltpu.make_async_copy(f_ref, fv, in_sem.at[1])
    t_copy = pltpu.make_async_copy(t_ref, tv, in_sem.at[2])
    x_copy.start()
    f_copy.start()
    t_copy.start()

    hops = [8 - (u + 1) // 2 if u % 2 else 8 + u // 2 for u in range(NZ)]
    peers = [lax.rem(z + dz, NZ) * 2 + at for dz in hops for at in (1 - core, core)][:-1]

    pq = ((x, y), (y, x))

    def ch_at(par, p, q):
        return q * 4 + p if par == 0 else p * 4 + q

    barrier = pltpu.get_barrier_semaphore()

    for peer in peers:
        pl.semaphore_signal(barrier, inc=1, device_id={"lat": peer}, device_id_type=MESH)
    for d in range(1, 4):
        for par in range(2):
            p, q = pq[par]
            pl.semaphore_signal(
                barrier, inc=1, device_id={"ch": ch_at(par, lax.rem(p + d, 4), q)}, device_id_type=MESH
            )

    dst = lax.broadcasted_iota(jnp.int32, (128, 96), 0)
    src = lax.broadcasted_iota(jnp.int32, (128, 96), 1)
    one = jnp.ones_like(dst)
    zero = jnp.zeros_like(dst)
    bc = (
        jnp.where(dst >= SLAB, one, zero)
        + jnp.where(dst >= 2 * SLAB, one, zero)
        + jnp.where(dst >= 3 * SLAB, one, zero)
    )
    k = dst - SLAB * bc
    south = jnp.where(lat >= NLATDEV // 2, 1, 0)
    k = k + south * (SLAB - 1 - 2 * k)
    want = (bc // 2) * (2 * SLAB) + 2 * k + bc % 2
    hit = jnp.logical_and(want == src, dst < 4 * SLAB)
    perm = jnp.where(hit, 1.0, 0.0).astype(bf16)
    xs[4 * SLAB :, :] = jnp.zeros((8, 2 * FP), f32)
    xs[:, NLON:] = jnp.zeros((96, 2 * FP - NLON), f32)
    x_copy.wait()
    for i in range(2 * SLAB):
        xs[2 * i : 2 * i + 2, :NLON] = xv[i // SLAB, i % SLAB].astype(f32)
    whole = xs[...]
    first = whole[:, :FP]
    second = pltpu.roll(whole, 2 * FP - FOLD, 1)[:, :FP]
    xp = [
        jnp.dot(perm, val.astype(bf16), preferred_element_type=f32).astype(bf16)
        for val in (first + second, first - second)
    ]

    f_copy.wait()

    def rows_of(i, par):
        return lax.dot_general(fv[i], xp[par], NT, preferred_element_type=f32)

    wide = lax.broadcasted_iota(jnp.int32, (NLATDEV * 8, 128), 1)
    spare = jnp.logical_and(wide >= 4 * SLAB, wide < 5 * SLAB)

    def transform(g):
        if g == 0:
            extra[...] = rows_of(4, 0) + rows_of(5, 1)
        if g < 2:
            halves = []
            for par in range(2):
                own = rows_of(2 * g + par, par)
                moved = pltpu.roll(extra[...], (4 - (2 * g + par)) * SLAB, 1)
                halves.append(jnp.where(spare, moved, own).reshape(NLATDEV, 8, 128))
            sb[g] = jnp.stack(halves, axis=1).astype(bf16)
        else:
            sb[g, :, 0] = rows_of(6, 1).reshape(NLATDEV, 8, 128).astype(bf16)
        rb[g, lat] = sb[g, lat]

    def z_part(g):
        return (slice(None), slice(None)) if g < 2 else (0, pl.ds(0, 4))

    def z_copy(g, dest):
        return pltpu.make_async_remote_copy(
            src_ref=sb.at[(g, dest) + z_part(g)],
            dst_ref=rb.at[(g, lat) + z_part(g)],
            send_sem=z_send.at[g],
            recv_sem=z_recv.at[g],
            device_id={"lat": dest},
            device_id_type=MESH,
        )

    def z_all(g):
        every = (g, pl.ds(0, NLATDEV - 1)) + z_part(g)
        return pltpu.make_async_remote_copy(
            src_ref=sb.at[every],
            dst_ref=rb.at[every],
            send_sem=z_send.at[g],
            recv_sem=z_recv.at[g],
            device_id={"lat": peers[0]},
            device_id_type=MESH,
        )

    def ready_table(g):
        for par in range(2):
            c = 2 * g + par
            q = pq[par][1]
            tg[c, q] = jnp.zeros((4, LP, KP), bf16)
            for j in range(4):
                if j in CHUNKS[c]:
                    tg[c, q, j, :LBLK, :HALF] = tv[CHUNKS[c][j]]
                else:
                    for i in range(4):
                        tg[c, i, j] = jnp.zeros((LP, KP), bf16)

    def t_move(c, d, piece):
        p, q = pq[c % 2]
        part = tg.at[c, q, pl.ds(*piece)]
        return pltpu.make_async_remote_copy(
            src_ref=part,
            dst_ref=part,
            send_sem=t_send.at[c],
            recv_sem=t_recv.at[c],
            device_id={"ch": ch_at(c % 2, p, lax.rem(q + d, 4))},
            device_id_type=MESH,
        )

    def t_pass(c, d):
        p, q = pq[c % 2]
        origin, to = lax.rem(q + 4 - d, 4), lax.rem(q + d, 4)
        half = pl.ds(*pieces(c)[d // 2])
        return pltpu.make_async_remote_copy(
            src_ref=tg.at[c, origin, half],
            dst_ref=tg.at[c, origin, half],
            send_sem=t_send.at[c],
            recv_sem=t_last.at[c],
            device_id={"ch": ch_at(c % 2, p, to)},
            device_id_type=MESH,
        )

    def t_all(c, blocks, recv):
        p, q = pq[c % 2]
        part = tg.at[c, pl.ds(0, blocks), pl.ds(0, len(CHUNKS[c]))]
        return pltpu.make_async_remote_copy(
            src_ref=part,
            dst_ref=part,
            send_sem=t_send.at[c],
            recv_sem=recv.at[c],
            device_id={"ch": ch_at(c % 2, p, lax.rem(q + 1, 4))},
            device_id_type=MESH,
        )

    def p_move(c, d):
        p, q = pq[c % 2]
        return pltpu.make_async_remote_copy(
            src_ref=yp.at[c],
            dst_ref=wb.at[c, :, p],
            send_sem=p_send.at[c],
            recv_sem=p_recv.at[c],
            device_id={"ch": ch_at(c % 2, lax.rem(p + d, 4), q)},
            device_id_type=MESH,
        )

    def p_all(c):
        p, q = pq[c % 2]
        part = wb.at[c, :, pl.ds(0, 3)]
        return pltpu.make_async_remote_copy(
            src_ref=part,
            dst_ref=part,
            send_sem=p_send.at[c],
            recv_sem=p_recv.at[c],
            device_id={"ch": ch_at(c % 2, lax.rem(p + 1, 4), q)},
            device_id_type=MESH,
        )

    def o_move(c, to):
        p, q = pq[c % 2]
        return pltpu.make_async_remote_copy(
            src_ref=ob.at[c, to],
            dst_ref=orr.at[c, q],
            send_sem=o_send.at[c],
            recv_sem=o_recv.at[c],
            device_id={"ch": ch_at(c % 2, p, to)},
            device_id_type=MESH,
        )

    def o_all(c):
        p, q = pq[c % 2]
        return pltpu.make_async_remote_copy(
            src_ref=ob.at[c, pl.ds(0, 3)],
            dst_ref=orr.at[c, pl.ds(0, 3)],
            send_sem=o_send.at[c],
            recv_sem=o_recv.at[c],
            device_id={"ch": ch_at(c % 2, p, lax.rem(q + 1, 4))},
            device_id_type=MESH,
        )

    def send_table(g):
        for c in (2 * g, 2 * g + 1):
            for d in (1, 3):
                for piece in pieces(c):
                    t_move(c, d, piece).start()

    def pass_table(g):
        for c in (2 * g, 2 * g + 1):
            t_all(c, 2, t_recv).wait_recv()
            for d in (1, 3):
                t_pass(c, d).start()

    for g in range(GROUPS):
        transform(g)
        if g == 0:
            t_copy.wait()
            ready_table(0)
            pl.semaphore_wait(barrier, NLATDEV - 1 + 6)
        for peer in peers:
            z_copy(g, peer).start()
        if g:
            ready_table(g)
        send_table(g)

    for par in range(2):
        row = lax.broadcasted_iota(jnp.int32, (512, 512), 0)
        col = lax.broadcasted_iota(jnp.int32, (512, 512), 1)
        qq, pp = row // 128, (row // 32) % 4
        chan = ch_at(par, pp, qq)
        want = (
            ((row // 2) % 4) * 128
            + ((row // 16) % 2) * 64
            + chan * 4
            + ((row // 8) % 2) * 2
            + row % 2
        )
        pm[par] = jnp.where(want == col, 1.0, 0.0).astype(bf16)

    lane = lax.broadcasted_iota(jnp.int32, (16, 128), 1)

    top = lax.broadcasted_iota(jnp.int32, (8, 128), 0) < 4

    def collect(s):
        joined = jnp.zeros((8, 128), f32)
        for b in range(4):
            moved = pltpu.roll(rb[b // 2, s, b % 2].astype(f32), 128 - (4 - b) * SLAB, 1)
            inside = jnp.logical_and(lane[:8] >= SLAB * b, lane[:8] < SLAB * (b + 1))
            joined = jnp.where(inside, moved, joined)
        rl[s, 0] = joined

    def arrived(g, s):
        return (rl[s] if g == 2 else rb[g, s].astype(f32)).reshape(16, 128)

    def unpack(g):
        if g == 2:
            for s in range(NLATDEV):
                collect(s)
        z_all(g).wait_recv()
        if g == 2:
            for s in range(NLATDEV):
                rl[s, 1] = jnp.where(top, rb[g, s, 0].astype(f32), rl[s, 0])
        for b in range(4):
            acc = [[jnp.zeros((16, 128), f32) for _ in range(3)] for _ in range(2)]
            for s in range(NLATDEV // 2):
                north = arrived(g, s)
                other = arrived(g, NLATDEV - 1 - s)
                first = SLAB * s
                shift = (first - SLAB * b) % 128
                for i, val in enumerate((north + other, north - other)):
                    if shift:
                        val = pltpu.roll(val, shift, 1)
                    for t in range(first // 128, (first + SLAB - 1) // 128 + 1):
                        lo, hi = first - 128 * t, first + SLAB - 128 * t
                        inside = jnp.logical_and(lane >= lo, lane < hi)
                        acc[i][t] = jnp.where(inside, val, acc[i][t])
            for par in range(2):
                for i in range(2):
                    for t in range(3):
                        yf[par, i, b, :, 128 * t : 128 * t + 128] = acc[i][t][
                            8 * par : 8 * par + 8
                        ]
        for par in range(2):
            c = 2 * g + par
            block = yf[par].reshape(2, 32, KP).astype(bf16)
            yp[c] = block
            wb[c, :, pq[par][0]] = block
            for d in (1, 3, 2):
                p_move(c, d).start()

    rows = lax.broadcasted_iota(jnp.int32, (LP, 128), 0)
    lanes = lax.broadcasted_iota(jnp.int32, (LP, 128), 1)
    lane_slot = (lanes // 2) % 4

    def project(c):
        par = c % 2
        q = pq[par][1]
        t_all(c, 1, t_last).wait_recv()
        p_all(c).wait_recv()
        got = lax.dot_general(
            tg[c].reshape(16 * LP, KP),
            wb[c].reshape(256, KP),
            NT,
            preferred_element_type=f32,
        )
        same = rows % 2 == par
        for i in range(4):
            total = jnp.zeros((LP, 128), f32)
            for j in CHUNKS[c]:
                lo = (4 * i + j) * LP
                both = got[lo : lo + LP]
                val = jnp.where(same, both[:, :128], both[:, 128:])
                total = jnp.where(lane_slot == j, val, total)
            ob[c, i] = total.astype(bf16)

            @pl.when(q != i)
            def _(i=i):
                o_move(c, i).start()

        orr[c, q] = ob[c, q]

    def finish(c):
        par = c % 2
        o_all(c).wait_recv()
        full = jnp.concatenate([orr[c, i] for i in range(4)], axis=1)
        res = jnp.dot(full, pm[par], preferred_element_type=f32)
        for j, local in CHUNKS[c].items():
            ov[local] = res[:LBLK, 128 * j : 128 * j + 128]
            pltpu.make_async_copy(ov.at[local], out_ref.at[local], out_sem.at[c]).start()

    def both(step, g):
        for par in range(2):
            step(2 * g + par)

    pass_table(0)
    pass_table(1)
    unpack(0)
    pass_table(2)
    unpack(1)
    unpack(2)
    for g in range(GROUPS):
        both(project, g)
    for g in range(GROUPS):
        z_all(g).wait_send()
    for c in range(2 * GROUPS):
        t_all(c, 3, t_recv).wait_send()
    for g in range(GROUPS):
        both(finish, g)
    for c in range(2 * GROUPS):
        p_all(c).wait_send()
        o_all(c).wait_send()
        whole = pl.ds(0, len(CHUNKS[c]))
        pltpu.make_async_copy(ov.at[whole], out_ref.at[whole], out_sem.at[c]).wait()


def shards(fields, table):
    fourier = jnp.asarray(fourier_rows())
    bf16, f32 = jnp.bfloat16, jnp.float32
    dma = pltpu.SemaphoreType.DMA
    chunks = 2 * GROUPS
    return pl.pallas_call(
        kernel,
        out_shape=jax.ShapeDtypeStruct((SLAB, LBLK, 128), f32),
        in_specs=[
            pl.BlockSpec(memory_space=pl.ANY),
            pl.BlockSpec(memory_space=pl.ANY),
            pl.BlockSpec(memory_space=pl.ANY),
        ],
        out_specs=pl.BlockSpec(memory_space=pl.ANY),
        scratch_shapes=[
            pltpu.VMEM((2, SLAB, 2, NLON), bf16),
            pltpu.VMEM((96, 2 * FP), f32),
            pltpu.VMEM((len(SENT), NLATDEV * 8, FP), bf16),
            pltpu.VMEM((SLAB, LBLK, HALF), bf16),
            pltpu.VMEM((NLATDEV * 8, 128), f32),
            pltpu.VMEM((GROUPS, NLATDEV, 2, 8, 128), bf16),
            pltpu.VMEM((GROUPS, NLATDEV, 2, 8, 128), bf16),
            pltpu.VMEM((NLATDEV, 2, 8, 128), f32),
            pltpu.VMEM((chunks, 4, 4, LP, KP), bf16),
            pltpu.VMEM((2, 2, 4, 8, KP), f32),
            pltpu.VMEM((chunks, 2, 32, KP), bf16),
            pltpu.VMEM((chunks, 2, 4, 32, KP), bf16),
            pltpu.VMEM((chunks, 4, LP, 128), bf16),
            pltpu.VMEM((chunks, 4, LP, 128), bf16),
            pltpu.VMEM((2, 512, 512), bf16),
            pltpu.VMEM((SLAB, LBLK, 128), f32),
            dma((3,)),
            dma((GROUPS,)),
            dma((GROUPS,)),
            dma((chunks,)),
            dma((chunks,)),
            dma((chunks,)),
            dma((chunks,)),
            dma((chunks,)),
            dma((chunks,)),
            dma((chunks,)),
            dma((chunks,)),
        ],
        compiler_params=pltpu.CompilerParams(
            collective_id=0, has_side_effects=True, vmem_limit_bytes=62 << 20
        ),
    )(fields, fourier, table)


def solution(mesh):
    return jax.shard_map(
        shards,
        mesh=mesh,
        in_specs=(P(None, "lat", "ch", None), P("lat", "ch", None)),
        out_specs=P("lat", "ch", None),
        check_vma=False,
    )
```
